32 devices in a mesh: slab: 16 (over z, y, x), sect: 2 (over core).
Axes of the slice: x: 2, y: 2, z: 4, core: 2. Of those that a mesh axis runs over, the one named last changes fastest.
Arguments:
- fields: float32 [2, 2, 2048, 2048], P(None, None, 'slab'), may hold values from -6 to 6
- region_ids: int32 [2, 2048, 2048], P('sect', 'slab'), may hold values from 0 to 15
- index_offsets: float32 [2, 16], replicated, may hold values from -0.002 to 0.002
- step_lengths: float32 [2], replicated, may hold values from 500 to 2000
- wave_numbers: float32 [2], replicated, may hold values from 0.5 to 2
- zone_ids: int32 [2048, 2048], P('slab'), may hold values from 0 to 31
- zone_phases: float32 [2, 32], replicated, may hold values from -3.140625 to 3.140625
Outputs:
- propagated: float32 [2, 2, 2048, 2048], P('sect', None, 'slab')
The draws below stay inside these ranges and needn't reach their ends.
All inputs are finite; a program needn't handle non-finite values.
Results may differ from the reference program's by a relative error of at most 0.00023.
Values sent between devices are 32-bit elements; how exact they have to be, the bound alone decides.
No kernel may reach another device: no remote copies, remote signals or barrier semaphores. Data moves between devices by JAX's collectives and lax.ppermute only.
A program may use at most 64 MiB of HBM per device.

```python
import math
import jax
import jax.numpy as jnp
from jax import lax

N = 2048
N1 = 16
N2 = 128
FIELDS = 2
STEPS = 2
REGIONS = 16
ZONES = 32
SECTIONS = 2


def draw_zone_ids(key, part):
    keys = jax.random.split(key, 3)
    centre_row = jax.random.randint(keys[0], (), N // 4, 3 * N // 4)
    centre_column = jax.random.randint(keys[1], (), N // 4, 3 * N // 4)
    cycle_width = jax.random.randint(keys[2], (), N * N // (4 * ZONES), N * N // (2 * ZONES))
    coords = jnp.arange(N, dtype=jnp.int32)
    row_offset = coords - centre_row
    column_offset = coords - centre_column
    radius = row_offset[:, None] * row_offset[:, None] + column_offset[None, :] * column_offset[None, :]
    return jnp.minimum(radius // cycle_width, ZONES - 1).astype(jnp.int32)


def with_ends(array, key, smallest, high):
    place = [jax.random.randint(jax.random.fold_in(key, axis), (), 0, length) for axis, length in enumerate(array.shape)]
    longest = array.shape.index(max(array.shape))
    beside = place[:longest] + [(place[longest] + 1) % array.shape[longest]] + place[longest + 1:]
    return array.at[tuple(place)].set(smallest).at[tuple(beside)].set(high)


def level_of(rng, extent, shards, least, high):
    level, own = 1.0, jax.random.fold_in(rng, 6)
    for axis_at, shards_of in shards:
        draws = jnp.exp(jax.random.uniform(jax.random.fold_in(own, axis_at), (shards_of,), jnp.float32, least / len(shards), high / len(shards)))
        level = level * jnp.repeat(draws, extent[axis_at] // shards_of).reshape([-1 if axis == axis_at else 1 for axis in range(len(extent))])
    return level


def centred(key, shape, scale, most, pieces=(), kind=jnp.bfloat16):
    array = jax.random.normal(key, shape, jnp.float32) * scale
    if len(pieces) > 0:
        array = level_of(key, shape, pieces, -0.22, 0.18) * array
    return jnp.clip(array, min=-most, max=most).astype(kind)


def setup_inputs(seed: int = 0) -> dict:
    seeds = jax.random.split(jax.random.key(seed), 8)
    return {
        "fields": centred(seeds[0], (FIELDS, 2, N, N), 1.0, 6.0, ((2, 16),), jnp.float32),
        "region_ids": with_ends(jax.random.randint(seeds[1], (SECTIONS, N, N), 0, REGIONS), jax.random.fold_in(seeds[1], 1), 0, REGIONS - 1).astype(jnp.int32),
        "index_offsets": jnp.clip(jax.random.uniform(seeds[2], (SECTIONS, REGIONS), jnp.float32, -0.002, 0.002), -0.002, 0.002),
        "step_lengths": jnp.clip(jax.random.uniform(seeds[3], (SECTIONS,), jnp.float32, 500.0, 2000.0), 500.0, 2000.0),
        "wave_numbers": jnp.clip(jnp.exp(jax.random.uniform(seeds[4], (FIELDS,), jnp.float32, math.log(0.5), math.log(2.0))), 0.5, 2.0),
        "zone_ids": draw_zone_ids(jax.random.fold_in(seeds[7], 71), 0),
        "zone_phases": jnp.clip(jax.random.uniform(seeds[6], (FIELDS, ZONES), jnp.float32, -3.140625, 3.140625), -3.140625, 3.140625),
    }


HIGHEST = lax.Precision.HIGHEST


def make_tables(first_len, second_len):
    total_len = first_len * second_len
    first_index = jnp.arange(first_len, dtype=jnp.int32)
    second_index = jnp.arange(second_len, dtype=jnp.int32)
    first_angle = ((first_index[:, None] * first_index[None, :]) % first_len).astype(jnp.float32) * (2.0 * math.pi / first_len)
    twist_angle = (first_index[:, None] * second_index[None, :]).astype(jnp.float32) * (2.0 * math.pi / total_len)
    second_angle = ((second_index[:, None] * second_index[None, :]) % second_len).astype(jnp.float32) * (2.0 * math.pi / second_len)
    position = jnp.arange(total_len, dtype=jnp.int32)
    frequency = position // second_len + first_len * (position % second_len)
    spread = jnp.sin(frequency.astype(jnp.float32) * (math.pi / total_len)) ** 2
    return (jnp.cos(first_angle), jnp.sin(first_angle), jnp.cos(twist_angle), jnp.sin(twist_angle), jnp.cos(second_angle), jnp.sin(second_angle), spread)


def left_apply(matrix, values):
    return jnp.einsum("kn,...nm->...km", matrix, values, precision=HIGHEST)


def right_apply(values, matrix):
    return jnp.einsum("...kn,nm->...km", values, matrix, precision=HIGHEST)


def forward(real_part, imaginary_part, tables):
    cos_one, sin_one, cos_twist, sin_twist, cos_two, sin_two = tables[:6]
    full_shape = real_part.shape
    grid_shape = full_shape[:-1] + (cos_one.shape[0], cos_two.shape[0])
    grid_real = real_part.reshape(grid_shape)
    grid_imaginary = imaginary_part.reshape(grid_shape)
    mixed_real = left_apply(cos_one, grid_real) + left_apply(sin_one, grid_imaginary)
    mixed_imaginary = left_apply(cos_one, grid_imaginary) - left_apply(sin_one, grid_real)
    turned_real = mixed_real * cos_twist + mixed_imaginary * sin_twist
    turned_imaginary = mixed_imaginary * cos_twist - mixed_real * sin_twist
    spectrum_real = right_apply(turned_real, cos_two) + right_apply(turned_imaginary, sin_two)
    spectrum_imaginary = right_apply(turned_imaginary, cos_two) - right_apply(turned_real, sin_two)
    return spectrum_real.reshape(full_shape), spectrum_imaginary.reshape(full_shape)


def backward(real_part, imaginary_part, tables):
    cos_one, sin_one, cos_twist, sin_twist, cos_two, sin_two = tables[:6]
    full_shape = real_part.shape
    grid_shape = full_shape[:-1] + (cos_one.shape[0], cos_two.shape[0])
    inverse_count = 1.0 / (cos_one.shape[0] * cos_two.shape[0])
    grid_real = real_part.reshape(grid_shape)
    grid_imaginary = imaginary_part.reshape(grid_shape)
    turned_real = right_apply(grid_real, cos_two) - right_apply(grid_imaginary, sin_two)
    turned_imaginary = right_apply(grid_imaginary, cos_two) + right_apply(grid_real, sin_two)
    mixed_real = turned_real * cos_twist - turned_imaginary * sin_twist
    mixed_imaginary = turned_imaginary * cos_twist + turned_real * sin_twist
    plain_real = left_apply(cos_one, mixed_real) - left_apply(sin_one, mixed_imaginary)
    plain_imaginary = left_apply(cos_one, mixed_imaginary) + left_apply(sin_one, mixed_real)
    return (plain_real * inverse_count).reshape(full_shape), (plain_imaginary * inverse_count).reshape(full_shape)


def crank_factor(wave_number, length, spread):
    curvature = -4.0 * spread[None, :] / (wave_number[:, None] * wave_number[:, None])
    stiffness = wave_number[:, None] * length * 0.25
    front_part = 1.0 + 0.25 * curvature
    cross_part = stiffness * curvature
    magnitude = front_part * front_part + cross_part * cross_part
    factor_real = (front_part * front_part - cross_part * cross_part) / magnitude
    factor_imaginary = 2.0 * front_part * cross_part / magnitude
    return factor_real[:, None, :], factor_imaginary[:, None, :]


def half_step(real_part, imaginary_part, factor_real, factor_imaginary, tables):
    spectrum_real, spectrum_imaginary = forward(real_part, imaginary_part, tables)
    scaled_real = spectrum_real * factor_real - spectrum_imaginary * factor_imaginary
    scaled_imaginary = spectrum_real * factor_imaginary + spectrum_imaginary * factor_real
    return backward(scaled_real, scaled_imaginary, tables)


def apply_screen(real_part, imaginary_part, phase):
    cosine = jnp.cos(phase)
    sine_value = jnp.sin(phase)
    return real_part * cosine - imaginary_part * sine_value, real_part * sine_value + imaginary_part * cosine


def pick_values(labels, table):
    picked = jnp.zeros(table.shape[:-1] + labels.shape[-2:], jnp.float32)
    for entry in range(table.shape[-1]):
        picked = picked + jnp.where(labels == entry, table[..., entry][..., None, None], 0.0)
    return picked


def reference(fields, region_ids, index_offsets, step_lengths, wave_numbers, zone_ids, zone_phases):
    tables = make_tables(N1, N2)
    spread = tables[6]
    offsets = [pick_values(region_ids[section], index_offsets[section]) for section in range(SECTIONS)]

    def one_field(packed):
        state, wave_number, phases = packed
        wave_number = wave_number.reshape(1)
        lens = pick_values(zone_ids, phases)[None]
        real_part = state[0][None]
        imaginary_part = state[1][None]
        for section in range(SECTIONS):
            length = step_lengths[section]
            factor_real, factor_imaginary = crank_factor(wave_number, length, spread)
            for step_index in range(STEPS):
                phase = wave_number[:, None, None] * length * offsets[section][None]
                if section == SECTIONS - 1 and step_index == 0:
                    phase = phase + lens
                real_part, imaginary_part = apply_screen(real_part, imaginary_part, phase)
                real_part, imaginary_part = half_step(real_part, imaginary_part, factor_real, factor_imaginary, tables)
                real_part, imaginary_part = half_step(jnp.swapaxes(real_part, 1, 2), jnp.swapaxes(imaginary_part, 1, 2), factor_real, factor_imaginary, tables)
                real_part = jnp.swapaxes(real_part, 1, 2)
                imaginary_part = jnp.swapaxes(imaginary_part, 1, 2)
        return jnp.concatenate([real_part, imaginary_part], axis=0)

    return lax.map(one_field, (fields, wave_numbers, zone_phases))
```

```python
import math
import jax
import jax.numpy as jnp
from jax import lax
from jax.sharding import PartitionSpec as P

STEPS = 2
BLOCK = 128
HIGHEST = lax.Precision.HIGHEST


def c_mul(a, b):
    return a[0] * b[0] - a[1] * b[1], a[0] * b[1] + a[1] * b[0]


def c_add(a, b):
    return a[0] + b[0], a[1] + b[1]


def c_div(a, b):
    size = b[0] * b[0] + b[1] * b[1]
    return (a[0] * b[0] + a[1] * b[1]) / size, (a[1] * b[0] - a[0] * b[1]) / size


def c_sqrt(a):
    size = jnp.sqrt(a[0] * a[0] + a[1] * a[1])
    real = jnp.sqrt(0.5 * (size + a[0]))
    return real, 0.5 * a[1] / real


def c_power(theta, count):
    size = jnp.exp(-theta[0] * count)
    angle = theta[1] * count
    return size * jnp.cos(angle), -size * jnp.sin(angle)


def scalars(number, length):
    sigma = number * length * 0.25
    size = 0.0625 + sigma * sigma
    square = number * number / size
    z = (-0.0625 * square, -0.25 * sigma * square)
    sinh = c_sqrt(z)
    cosh = c_sqrt((1.0 + z[0], z[1]))
    small = c_add(sinh, c_div(z, (1.0 + cosh[0], cosh[1])))
    theta = (
        jnp.log1p(2.0 * small[0] + small[0] * small[0] + small[1] * small[1]),
        2.0 * jnp.arctan2(small[1], 1.0 + small[0]),
    )
    front = (-2.0 * sigma * sigma / size, -0.5 * sigma / size)
    gamma = c_mul(front, c_div(sinh, cosh))
    alpha = ((0.0625 - sigma * sigma) / size, 0.5 * sigma / size)
    return theta, gamma, c_mul(alpha, alpha)


def closure(theta, total):
    power = c_power(theta, float(total))
    return c_div((jnp.ones_like(power[0]), jnp.zeros_like(power[0])), (1.0 - power[0], -power[1]))


def toeplitz(theta, gamma, count):
    index = jnp.arange(count, dtype=jnp.int32)
    apart = jnp.abs(index[:, None] - index[None, :])
    real, imaginary = c_mul(gamma, c_power(theta, apart.astype(jnp.float32)))
    return jnp.where(apart == 0, 1.0, 0.0) + real, imaginary


def circulant(theta, size, blocks):
    index = jnp.arange(blocks, dtype=jnp.int32)
    apart = jnp.mod(index[:, None] - index[None, :] - 1, blocks).astype(jnp.float32)
    return c_mul(closure(theta, size * blocks), c_power(theta, apart * size))


def c_ein(spec, a, b):
    def one(x, y):
        return jnp.einsum(spec, x, y, precision=HIGHEST)

    return one(a[0], b[0]) - one(a[1], b[1]), one(a[0], b[1]) + one(a[1], b[0])


def spans(theta, gamma, count):
    index = jnp.arange(count, dtype=jnp.int32).astype(jnp.float32)
    weight_left = c_mul(gamma, c_power(theta, count - 1 - index))
    weight_right = c_mul(gamma, c_power(theta, index))
    reach_left = c_power(theta, index + 1)
    reach_right = c_power(theta, count - index)
    return weight_left, weight_right, reach_left, reach_right


def row_solve(x, theta, gamma):
    shape = x[0].shape
    blocks = shape[-1] // BLOCK
    x = tuple(part.reshape(shape[:-1] + (blocks, BLOCK)) for part in x)
    weight_left, weight_right, reach_left, reach_right = spans(theta, gamma, BLOCK)
    ring = circulant(theta, BLOCK, blocks)
    y = c_ein("...bi,ij->...bj", x, toeplitz(theta, gamma, BLOCK))
    left = c_ein("...b,cb->...c", c_ein("...bi,i->...b", x, weight_left), ring)
    right = c_ein("...b,bc->...c", c_ein("...bi,i->...b", x, weight_right), ring)
    y = c_add(y, c_ein("...b,i->...bi", left, reach_left))
    y = c_add(y, c_ein("...b,i->...bi", right, reach_right))
    return tuple(part.reshape(shape) for part in y)


def pick_values(labels, table):
    picked = jnp.zeros(labels.shape, jnp.float32)
    for entry in range(table.shape[-1]):
        picked = picked + jnp.where(labels == entry, table[entry], 0.0)
    return picked


def column_local(x, theta, gamma, rows):
    weight_left, weight_right, _, _ = spans(theta, gamma, rows)
    y = c_ein("ij,jm->im", toeplitz(theta, gamma, rows), x)
    return y, c_ein("i,im->m", weight_left, x), c_ein("i,im->m", weight_right, x)


def reach(y, left, right, theta, gamma, rows):
    _, _, reach_left, reach_right = spans(theta, gamma, rows)
    y = c_add(y, c_ein("i,m->im", reach_left, left))
    return c_add(y, c_ein("i,m->im", reach_right, right))


def payload(y, left, right, screen, theta, gamma, rows):
    weight_left, weight_right, reach_left, reach_right = spans(theta, gamma, rows)
    z = c_mul(screen, y)
    parts = [left, right, c_ein("i,im->m", weight_left, z), c_ein("i,im->m", weight_right, z)]
    for weight, other in ((weight_left, reach_left), (weight_left, reach_right), (weight_right, reach_left)):
        parts.append(c_ein("i,im->m", c_mul(weight, other), screen))
    return jnp.stack([half for part in parts for half in part])


def exchange(packed, theta, rows):
    peers = lax.axis_size("slab")
    width = packed.shape[-1] // peers
    sent = jnp.swapaxes(packed.reshape(packed.shape[0], peers, width), 0, 1)
    held = lax.all_to_all(sent, "slab", 0, 0, tiled=True)
    one = [(held[:, 2 * i], held[:, 2 * i + 1]) for i in range(7)]
    ring = circulant(theta, rows, peers)
    left = c_ein("cb,bm->cm", ring, one[0])
    right = c_ein("bc,bm->cm", ring, one[1])
    next_left = c_add(one[2], c_add(c_mul(one[4], left), c_mul(one[5], right)))
    next_right = c_add(one[3], c_add(c_mul(one[6], left), c_mul(one[4], right)))
    next_left = c_ein("cb,bm->cm", ring, next_left)
    next_right = c_ein("bc,bm->cm", ring, next_right)
    back = jnp.stack([half for part in (left, right, next_left, next_right) for half in part], axis=1)
    back = lax.all_to_all(back, "slab", 0, 0, tiled=True)
    back = jnp.swapaxes(back, 0, 1).reshape(8, peers * width)
    return [(back[2 * i], back[2 * i + 1]) for i in range(4)]


def shards(fields, region_ids, index_offsets, step_lengths, wave_numbers, zone_ids, zone_phases):
    mine = lax.axis_index("sect")
    other = lax.ppermute(region_ids, "sect", [(0, 1), (1, 0)])
    labels = [jnp.where(mine == s, region_ids[0], other[0]) for s in range(2)]
    field = lax.dynamic_index_in_dim(fields, mine, 0, False)
    number = lax.dynamic_index_in_dim(wave_numbers, mine, 0, False)
    phases = lax.dynamic_index_in_dim(zone_phases, mine, 0, False)
    rows = field.shape[1]
    u = (field[0], field[1])
    lens = (pick_values(zone_ids, jnp.cos(phases)), pick_values(zone_ids, jnp.sin(phases)))
    for section in range(2):
        theta, gamma, turn = scalars(number, step_lengths[section])
        phase = number * step_lengths[section] * index_offsets[section]
        table = c_mul(turn, (jnp.cos(phase), jnp.sin(phase)))
        screen = tuple(pick_values(labels[section], half) for half in table)
        u = c_mul(u, screen)
        if section == 1:
            u = c_mul(u, lens)
        u, left, right = column_local(row_solve(u, theta, gamma), theta, gamma, rows)
        sent = payload(u, left, right, screen, theta, gamma, rows)
        back = exchange(sent, theta, rows)
        u = reach(u, back[0], back[1], theta, gamma, rows)
        u, _, _ = column_local(row_solve(c_mul(u, screen), theta, gamma), theta, gamma, rows)
        left = row_solve(back[2], theta, gamma)
        right = row_solve(back[3], theta, gamma)
        u = reach(u, left, right, theta, gamma, rows)
    return jnp.stack(u)[None]


def solution(mesh):
    return jax.shard_map(
        shards,
        mesh=mesh,
        in_specs=(
            P(None, None, "slab", None),
            P("sect", "slab", None),
            P(),
            P(),
            P(),
            P("slab", None),
            P(),
        ),
        out_specs=P("sect", None, "slab", None),
        check_vma=False,
    )
```

```python
from functools import partial

import jax
import jax.numpy as jnp
from jax import lax
from jax.experimental import pallas as pl
from jax.experimental.pallas import tpu as pltpu
from jax.sharding import PartitionSpec as P

STEPS = 2
BLOCK = 128
INTERPRET = False
HIGHEST = lax.Precision.HIGHEST


def c_mul(a, b):
    return a[0] * b[0] - a[1] * b[1], a[0] * b[1] + a[1] * b[0]


def c_add(a, b):
    return a[0] + b[0], a[1] + b[1]


def c_div(a, b):
    size = b[0] * b[0] + b[1] * b[1]
    return (a[0] * b[0] + a[1] * b[1]) / size, (a[1] * b[0] - a[0] * b[1]) / size


def c_sqrt(a):
    size = jnp.sqrt(a[0] * a[0] + a[1] * a[1])
    real = jnp.sqrt(0.5 * (size + a[0]))
    return real, 0.5 * a[1] / real


def c_power(theta, count):
    size = jnp.exp(-theta[0] * count)
    angle = theta[1] * count
    return size * jnp.cos(angle), -size * jnp.sin(angle)


def scalars(number, length):
    sigma = number * length * 0.25
    size = 0.0625 + sigma * sigma
    square = number * number / size
    z = (-0.0625 * square, -0.25 * sigma * square)
    sinh = c_sqrt(z)
    cosh = c_sqrt((1.0 + z[0], z[1]))
    small = c_add(sinh, c_div(z, (1.0 + cosh[0], cosh[1])))
    theta = (
        jnp.log1p(2.0 * small[0] + small[0] * small[0] + small[1] * small[1]),
        2.0 * jnp.arctan2(small[1], 1.0 + small[0]),
    )
    front = (-2.0 * sigma * sigma / size, -0.5 * sigma / size)
    gamma = c_mul(front, c_div(sinh, cosh))
    alpha = ((0.0625 - sigma * sigma) / size, 0.5 * sigma / size)
    return theta, gamma, c_mul(alpha, alpha)


def closure(theta, total):
    power = c_power(theta, float(total))
    return c_div((jnp.ones_like(power[0]), jnp.zeros_like(power[0])), (1.0 - power[0], -power[1]))


def toeplitz(theta, gamma, count):
    index = jnp.arange(count, dtype=jnp.int32)
    apart = jnp.abs(index[:, None] - index[None, :])
    real, imaginary = c_mul(gamma, c_power(theta, apart.astype(jnp.float32)))
    return jnp.where(apart == 0, 1.0, 0.0) + real, imaginary


def circulant(theta, size, blocks):
    index = jnp.arange(blocks, dtype=jnp.int32)
    apart = jnp.mod(index[:, None] - index[None, :] - 1, blocks).astype(jnp.float32)
    return c_mul(closure(theta, size * blocks), c_power(theta, apart * size))


def c_ein(spec, a, b):
    def one(x, y):
        return jnp.einsum(spec, x, y, precision=HIGHEST)

    return one(a[0], b[0]) - one(a[1], b[1]), one(a[0], b[1]) + one(a[1], b[0])


def spans(theta, gamma, count):
    index = jnp.arange(count, dtype=jnp.int32).astype(jnp.float32)
    weight_left = c_mul(gamma, c_power(theta, count - 1 - index))
    weight_right = c_mul(gamma, c_power(theta, index))
    reach_left = c_power(theta, index + 1)
    reach_right = c_power(theta, count - index)
    return weight_left, weight_right, reach_left, reach_right


def row_solve(x, theta, gamma):
    shape = x[0].shape
    blocks = shape[-1] // BLOCK
    x = tuple(part.reshape(shape[:-1] + (blocks, BLOCK)) for part in x)
    weight_left, weight_right, reach_left, reach_right = spans(theta, gamma, BLOCK)
    ring = circulant(theta, BLOCK, blocks)
    y = c_ein("...bi,ij->...bj", x, toeplitz(theta, gamma, BLOCK))
    left = c_ein("...b,cb->...c", c_ein("...bi,i->...b", x, weight_left), ring)
    right = c_ein("...b,bc->...c", c_ein("...bi,i->...b", x, weight_right), ring)
    y = c_add(y, c_ein("...b,i->...bi", left, reach_left))
    y = c_add(y, c_ein("...b,i->...bi", right, reach_right))
    return tuple(part.reshape(shape) for part in y)


def pick_values(labels, table):
    picked = jnp.zeros(labels.shape, jnp.float32)
    for entry in range(table.shape[-1]):
        picked = picked + jnp.where(labels == entry, table[entry], 0.0)
    return picked


def column_local(x, theta, gamma, rows):
    weight_left, weight_right, _, _ = spans(theta, gamma, rows)
    y = c_ein("ij,jm->im", toeplitz(theta, gamma, rows), x)
    return y, c_ein("i,im->m", weight_left, x), c_ein("i,im->m", weight_right, x)


def reach(y, left, right, theta, gamma, rows):
    _, _, reach_left, reach_right = spans(theta, gamma, rows)
    y = c_add(y, c_ein("i,m->im", reach_left, left))
    return c_add(y, c_ein("i,m->im", reach_right, right))


def payload(y, left, right, screen, theta, gamma, rows):
    weight_left, weight_right, reach_left, reach_right = spans(theta, gamma, rows)
    z = c_mul(screen, y)
    parts = [left, right, c_ein("i,im->m", weight_left, z), c_ein("i,im->m", weight_right, z)]
    for weight, other in ((weight_left, reach_left), (weight_left, reach_right), (weight_right, reach_left)):
        parts.append(c_ein("i,im->m", c_mul(weight, other), screen))
    return jnp.stack([half for part in parts for half in part])


def exchange(packed, theta, rows):
    peers = lax.axis_size("slab")
    width = packed.shape[-1] // peers
    sent = jnp.swapaxes(packed.reshape(packed.shape[0], peers, width), 0, 1)
    held = lax.all_to_all(sent, "slab", 0, 0, tiled=True)
    one = [(held[:, 2 * i], held[:, 2 * i + 1]) for i in range(7)]
    ring = circulant(theta, rows, peers)
    left = c_ein("cb,bm->cm", ring, one[0])
    right = c_ein("bc,bm->cm", ring, one[1])
    next_left = c_add(one[2], c_add(c_mul(one[4], left), c_mul(one[5], right)))
    next_right = c_add(one[3], c_add(c_mul(one[6], left), c_mul(one[4], right)))
    next_left = c_ein("cb,bm->cm", ring, next_left)
    next_right = c_ein("bc,bm->cm", ring, next_right)
    back = jnp.stack([half for part in (left, right, next_left, next_right) for half in part], axis=1)
    back = lax.all_to_all(back, "slab", 0, 0, tiled=True)
    back = jnp.swapaxes(back, 0, 1).reshape(8, peers * width)
    return [(back[2 * i], back[2 * i + 1]) for i in range(4)]


def shards(fields, region_ids, index_offsets, step_lengths, wave_numbers, zone_ids, zone_phases):
    mine = lax.axis_index("sect")
    other = lax.ppermute(region_ids, "sect", [(0, 1), (1, 0)])
    labels = [jnp.where(mine == s, region_ids[0], other[0]) for s in range(2)]
    field = lax.dynamic_index_in_dim(fields, mine, 0, False)
    number = lax.dynamic_index_in_dim(wave_numbers, mine, 0, False)
    phases = lax.dynamic_index_in_dim(zone_phases, mine, 0, False)
    rows = field.shape[1]
    u = (field[0], field[1])
    lens = (pick_values(zone_ids, jnp.cos(phases)), pick_values(zone_ids, jnp.sin(phases)))
    for section in range(2):
        theta, gamma, turn = scalars(number, step_lengths[section])
        phase = number * step_lengths[section] * index_offsets[section]
        table = c_mul(turn, (jnp.cos(phase), jnp.sin(phase)))
        screen = tuple(pick_values(labels[section], half) for half in table)
        u = c_mul(u, screen)
        if section == 1:
            u = c_mul(u, lens)
        u, left, right = column_local(row_solve(u, theta, gamma), theta, gamma, rows)
        sent = payload(u, left, right, screen, theta, gamma, rows)
        back = exchange(sent, theta, rows)
        u = reach(u, back[0], back[1], theta, gamma, rows)
        u, _, _ = column_local(row_solve(c_mul(u, screen), theta, gamma), theta, gamma, rows)
        left = row_solve(back[2], theta, gamma)
        right = row_solve(back[3], theta, gamma)
        u = reach(u, left, right, theta, gamma, rows)
    return jnp.stack(u)[None]


F32 = jnp.float32
BF16 = jnp.bfloat16
LHS_ROWS = 272
CHUNK = 32
VMEM_LIMIT = 56 * 1024 * 1024


def tile_of(value):
    return jnp.full((8, BLOCK), value, F32)


def grid_power(base, exponent, bits):
    real = jnp.ones(exponent.shape, F32)
    imaginary = jnp.zeros(exponent.shape, F32)
    for bit in range(bits):
        on = (exponent // (1 << bit)) % 2 == 1
        step = c_mul((real, imaginary), base)
        real = jnp.where(on, step[0], real)
        imaginary = jnp.where(on, step[1], imaginary)
        base = c_mul(base, base)
    return real, imaginary


def spread_to(pair, shape):
    return tuple(jnp.broadcast_to(part[0:1, 0:1], shape) for part in pair)


def prepare_kernel(total, number_ref, length_ref, offset_ref, zone_ref, matrix_ref, column_ref, row_ref):
    mine = lax.axis_index("sect")
    number = tile_of(number_ref[mine])
    tall = (BLOCK, BLOCK)
    place = lax.broadcasted_iota(jnp.int32, tall, 0)
    across = lax.broadcasted_iota(jnp.int32, tall, 1)
    lane = lax.broadcasted_iota(jnp.int32, (8, BLOCK), 1)
    lens = zone_ref[pl.ds(mine, 1), :]
    for section in range(2):
        length = tile_of(length_ref[section])
        sigma = number * length * 0.25
        size = 0.0625 + sigma * sigma
        square = number * number / size
        z = (-0.0625 * square, -0.25 * sigma * square)
        sinh = c_sqrt(z)
        cosh = c_sqrt((1.0 + z[0], z[1]))
        root = (cosh[0] - sinh[0], cosh[1] - sinh[1])
        base = c_mul(root, root)
        gamma = c_mul((-2.0 * sigma * sigma / size, -0.5 * sigma / size), c_div(sinh, cosh))
        alpha = ((0.0625 - sigma * sigma) / size, 0.5 * sigma / size)
        turn = c_mul(alpha, alpha)
        hop = base
        for _ in range(7):
            hop = c_mul(hop, hop)
        whole = hop
        for _ in range(total.bit_length() - 8):
            whole = c_mul(whole, whole)
        close = c_div((jnp.ones_like(whole[0]), jnp.zeros_like(whole[0])), (1.0 - whole[0], -whole[1]))
        wide = spread_to(base, tall)
        gain = spread_to(gamma, tall)
        real, imaginary = c_mul(gain, grid_power(wide, jnp.abs(place - across), 7))
        real = real + jnp.where(place == across, 1.0, 0.0)
        matrix_ref[section, 0:128, 0:128] = real
        matrix_ref[section, 0:128, 128:256] = -imaginary
        matrix_ref[section, 128:256, 0:128] = imaginary
        matrix_ref[section, 128:256, 128:256] = real
        ahead = grid_power(base, lane, 7)
        behind = grid_power(base, 127 - lane, 7)
        left = c_mul(gamma, behind)
        right = c_mul(gamma, ahead)
        zero = jnp.zeros((1, BLOCK), F32)
        rows = (left, right)
        for index, weight in enumerate(rows):
            matrix_ref[section, 256 + 2 * index : 257 + 2 * index, 0:128] = weight[0][0:1]
            matrix_ref[section, 256 + 2 * index : 257 + 2 * index, 128:256] = -weight[1][0:1]
            matrix_ref[section, 257 + 2 * index : 258 + 2 * index, 0:128] = weight[1][0:1]
            matrix_ref[section, 257 + 2 * index : 258 + 2 * index, 128:256] = weight[0][0:1]
        matrix_ref[section, 260:384, :] = jnp.zeros((124, 256), F32)
        phase = number * length * jnp.broadcast_to(offset_ref[section : section + 1, :], (8, BLOCK))
        screen = c_mul(turn, (jnp.cos(phase), jnp.sin(phase)))
        reach_left = c_mul(base, ahead)
        reach_right = c_mul(base, behind)
        listed = [screen[0], screen[1], jnp.broadcast_to(jnp.cos(lens), (8, BLOCK)), jnp.broadcast_to(jnp.sin(lens), (8, BLOCK))]
        listed += [reach_left[0], reach_left[1], reach_right[0], reach_right[1], hop[0], hop[1], close[0], close[1]]
        both = c_mul(gamma, hop)
        listed += [both[0], both[1]]
        for index, value in enumerate(listed):
            row_ref[section, 8 * index : 8 * index + 8, :] = value
        down = grid_power(wide, place, 7)
        up = grid_power(wide, 127 - place, 7)
        high = c_mul(wide, down)
        low = c_mul(wide, up)
        from_left = c_mul(gain, up)
        from_right = c_mul(gain, down)
        tables = [high, low, from_left, from_right, c_mul(from_left, low), c_mul(from_right, high)]
        for index, table in enumerate(tables):
            column_ref[section, 2 * index] = table[0]
            column_ref[section, 2 * index + 1] = table[1]


def split(value):
    high = value.astype(BF16)
    return high, (value - high.astype(F32)).astype(BF16)


def set_matrix(matrix_ref, section, factor_ref):
    high, low = split(matrix_ref[section, 0:LHS_ROWS, :])
    factor_ref[section, :, 0:256] = high
    factor_ref[section, :, 256:512] = low
    factor_ref[section, :, 512:768] = high


def put_operand(operand_ref, top, real, imaginary):
    size = real.shape[0]
    high, low = split(real)
    operand_ref[top : top + size, 0:128] = high
    operand_ref[top : top + size, 256:384] = low
    high, low = split(imaginary)
    operand_ref[top : top + size, 128:256] = high
    operand_ref[top : top + size, 384:512] = low


def multiply(factor_ref, section, operand_ref):
    high = operand_ref[:, 0:256]
    right = jnp.concatenate([high, high, operand_ref[:, 256:512]], axis=1)
    return lax.dot_general(factor_ref[section], right, (((1,), (1,)), ((), ())), preferred_element_type=F32)


def pick(table_ref, section, index, labels):
    table = jnp.broadcast_to(table_ref[section, 8 * index : 8 * index + 1, :], labels.shape)
    return jnp.take_along_axis(table, labels, axis=1, mode="promise_in_bounds")


def row_line(row_ref, section, index):
    return row_ref[section, 8 * index : 8 * index + 1, :]


def hop_of(row_ref, section):
    return (row_line(row_ref, section, 8), row_line(row_ref, section, 9)), (row_line(row_ref, section, 10), row_line(row_ref, section, 11))


def carries(get, put, count, hop, close):
    for reverse in (False, True):
        order = list(range(count))[:: -1 if reverse else 1]
        total = get(order[0], reverse)
        for index in order[1:]:
            total = c_add(c_mul(hop, total), get(index, reverse))
        carry = c_mul(close, total)
        for index in order:
            put(index, reverse, carry)
            carry = c_add(c_mul(hop, carry), get(index, reverse))


def scan_rows(edge_ref, carry_ref, row_ref, section, pairs):
    hop, close = hop_of(row_ref, section)

    def get(block, reverse):
        first = 2 if reverse else 0
        lanes = slice(128 * (block % 2), 128 * (block % 2) + 128)
        return tuple(edge_ref[block // 2, first + part : first + part + 1, lanes] for part in range(2))

    def put(block, reverse, value):
        first = 2 if reverse else 0
        for part in range(2):
            carry_ref[block, first + part : first + part + 1, :] = value[part]

    carries(get, put, 2 * pairs, hop, close)


def add_reach(column_ref, section, rows, value, left, right):
    high = (column_ref[section, 0, rows, :], column_ref[section, 1, rows, :])
    low = (column_ref[section, 2, rows, :], column_ref[section, 3, rows, :])
    return c_add(value, c_add(c_mul(high, left), c_mul(low, right)))


def row_pass(section, operand_ref, factor_ref, grid_ref, edge_ref, pair):
    out = multiply(factor_ref, section, operand_ref)
    grid_ref[pair] = out[0:256]
    edge_ref[pair] = out[256:264]


def column_pass(section, operand_ref, factor_ref, column_ref, carry_ref, grid_ref, pair):
    for half in range(2):
        lanes = slice(128 * half, 128 * half + 128)
        block = 2 * pair + half
        line = [carry_ref[block, part : part + 1, :] for part in range(4)]
        for top in range(0, BLOCK, CHUNK):
            rows = slice(top, top + CHUNK)
            value = (grid_ref[pair, rows, lanes], grid_ref[pair, top + 128 : top + 128 + CHUNK, lanes])
            value = add_reach(column_ref, section, rows, value, (line[0], line[1]), (line[2], line[3]))
            put_operand(operand_ref, 128 * half + top, *value)
    return multiply(factor_ref, section, operand_ref)


def pack_sums(section, value_ref, label_at, pair, row_ref, column_ref, ends, out_ref):
    for half in range(2):
        block = 2 * pair + half
        lanes = slice(128 * half, 128 * half + 128)
        sums = [jnp.zeros((8, BLOCK), F32) for _ in range(10)]
        for top in range(0, BLOCK, 8):
            rows = slice(top, top + 8)
            labels = label_at(half, rows)
            screen = (pick(row_ref, section, 0, labels), pick(row_ref, section, 1, labels))
            value = c_mul(screen, (value_ref[rows, lanes], value_ref[top + 128 : top + 136, lanes]))
            weights = [(column_ref[section, 2 * k, rows, :], column_ref[section, 2 * k + 1, rows, :]) for k in range(2, 6)]
            terms = (c_mul(weights[0], value), c_mul(weights[1], value), screen, c_mul(weights[2], screen), c_mul(weights[3], screen))
            for k, term in enumerate(terms):
                sums[2 * k] = sums[2 * k] + term[0]
                sums[2 * k + 1] = sums[2 * k + 1] + term[1]
        lines = [jnp.sum(part, axis=0, keepdims=True) for part in sums]
        both = c_mul((row_line(row_ref, section, 12), row_line(row_ref, section, 13)), (lines[4], lines[5]))
        out_ref[block, 0:4, :] = ends[0:4, lanes]
        for k, line in enumerate(lines[0:4] + list(both) + lines[6:10]):
            out_ref[block, 4 + k : 5 + k, :] = line
        out_ref[block, 14:16, :] = jnp.zeros((2, BLOCK), F32)


def line_solve(section, back_ref, small_ref, line_ref, edge_ref, matrix_ref, row_ref, blocks):
    small_ref[...] = jnp.zeros(small_ref.shape, F32)
    for block in range(blocks):
        for side in range(2):
            for part in range(2):
                row = 4 + 2 * side + part
                small_ref[8 * block + side : 8 * block + side + 1, 128 * part : 128 * part + 128] = back_ref[block, row : row + 1, :]
    high, low = split(small_ref[...])
    factor_high, factor_low = split(matrix_ref[section])

    def dot(a, b):
        return lax.dot_general(a, b, (((1,), (1,)), ((), ())), preferred_element_type=F32)

    out = dot(high, factor_high) + dot(low, factor_high) + dot(high, factor_low)
    line_ref[...] = out
    hop, close = hop_of(row_ref, section)
    wide = (8, BLOCK)
    hop = tuple(jnp.broadcast_to(part, wide) for part in hop)
    close = tuple(jnp.broadcast_to(part, wide) for part in close)
    reach_left = tuple(row_ref[section, 8 * k : 8 * k + 8, :] for k in (4, 5))
    reach_right = tuple(row_ref[section, 8 * k : 8 * k + 8, :] for k in (6, 7))

    def get(block, reverse):
        first = 258 if reverse else 256
        rows = slice(8 * block, 8 * block + 8)
        return tuple(jnp.broadcast_to(line_ref[rows, first + part : first + part + 1], wide) for part in range(2))

    def put(block, reverse, value):
        rows = slice(8 * block, 8 * block + 8)
        add = c_mul(reach_right if reverse else reach_left, value)
        line_ref[rows, 0:128] = line_ref[rows, 0:128] + add[0]
        line_ref[rows, 128:256] = line_ref[rows, 128:256] + add[1]

    carries(get, put, blocks, hop, close)


def line_at(line_ref, block):
    parts = []
    rows = pl.ds(pl.multiple_of(8 * block, 8), 8)
    for side in range(2):
        for part in range(2):
            parts.append(line_ref[rows, 128 * part : 128 * part + 128][side : side + 1])
    return (parts[0], parts[1]), (parts[2], parts[3])


def lanes_of(pair, half):
    return pl.ds(pl.multiple_of(256 * pair + 128 * half, 128), 128)


def first_kernel(pairs, field_any, own_any, other_any, matrix_ref, column_ref, row_ref, out_ref, sums_ref,
                 field_ref, label_ref, factor_ref, operand_ref, grid_ref, edge_ref, carry_ref, value_ref, sems):
    mine = lax.axis_index("sect")
    copy = pltpu.make_async_copy(field_any.at[mine], field_ref, sems.at[0])
    copy.start()

    @pl.when(mine == 0)
    def _():
        pltpu.make_async_copy(own_any.at[0], label_ref, sems.at[1]).start()

    @pl.when(mine != 0)
    def _():
        pltpu.make_async_copy(other_any.at[0], label_ref, sems.at[1]).start()

    set_matrix(matrix_ref, 0, factor_ref)
    copy.wait()
    pltpu.make_async_copy(own_any.at[0], label_ref, sems.at[1]).wait()

    def enter(pair, _):
        for half in range(2):
            for top in range(0, BLOCK, CHUNK):
                rows = slice(top, top + CHUNK)
                lanes = lanes_of(pair, half)
                labels = label_ref[rows, lanes]
                screen = (pick(row_ref, 0, 0, labels), pick(row_ref, 0, 1, labels))
                value = c_mul(screen, (field_ref[0, rows, lanes], field_ref[1, rows, lanes]))
                put_operand(operand_ref, 128 * half + top, *value)
        row_pass(0, operand_ref, factor_ref, grid_ref, edge_ref, pair)
        return 0

    lax.fori_loop(0, pairs, enter, 0)
    scan_rows(edge_ref, carry_ref, row_ref, 0, pairs)

    def leave(pair, _):
        value = column_pass(0, operand_ref, factor_ref, column_ref, carry_ref, grid_ref, pair)
        value_ref[...] = value[0:264]
        wide = pl.ds(pl.multiple_of(256 * pair, 256), 256)
        out_ref[0, :, wide] = value[0:128]
        out_ref[1, :, wide] = value[128:256]
        pack_sums(0, value_ref, lambda half, rows: label_ref[rows, lanes_of(pair, half)], pair, row_ref, column_ref,
                  value_ref[256:264, :], sums_ref)
        return 0

    lax.fori_loop(0, pairs, leave, 0)


def middle_kernel(peers, section, held_ref, row_ref, back_ref):
    hop, close = hop_of(row_ref, section)

    def line(peer, row):
        return held_ref[peer, row : row + 1, :], held_ref[peer, row + 1 : row + 2, :]

    def keep(first):
        def put(peer, reverse, value):
            row = first + (2 if reverse else 0)
            back_ref[peer, row : row + 1, :] = value[0]
            back_ref[peer, row + 1 : row + 2, :] = value[1]

        return put

    carries(lambda peer, reverse: line(peer, 2 if reverse else 0), keep(0), peers, hop, close)

    def later(peer, reverse):
        left = (back_ref[peer, 0:1, :], back_ref[peer, 1:2, :])
        right = (back_ref[peer, 2:3, :], back_ref[peer, 3:4, :])
        if reverse:
            return c_add(line(peer, 6), c_add(c_mul(line(peer, 12), left), c_mul(line(peer, 8), right)))
        return c_add(line(peer, 4), c_add(c_mul(line(peer, 8), left), c_mul(line(peer, 10), right)))

    carries(later, keep(4), peers, hop, close)


def take_in(section, pair, value_ref, label_ref, back_ref, column_ref, row_ref, operand_ref):
    for half in range(2):
        block = 2 * pair + half
        lanes = lanes_of(pair, half)
        line = [back_ref[block, part : part + 1, :] for part in range(4)]
        for top in range(0, BLOCK, CHUNK):
            rows = slice(top, top + CHUNK)
            value = (value_ref[0, rows, lanes], value_ref[1, rows, lanes])
            value = add_reach(column_ref, section, rows, value, (line[0], line[1]), (line[2], line[3]))
            labels = label_ref[rows, lanes]
            value = c_mul((pick(row_ref, section, 0, labels), pick(row_ref, section, 1, labels)), value)
            put_operand(operand_ref, 128 * half + top, *value)


def second_kernel(pairs, value_in, back_ref, own_any, other_any, zone_ref, matrix_ref, column_ref, row_ref, out_ref, sums_ref,
                  label_ref, factor_ref, operand_ref, grid_ref, edge_ref, carry_ref, value_ref, small_ref, line_ref, sems):
    mine = lax.axis_index("sect")

    @pl.when(mine == 0)
    def _():
        pltpu.make_async_copy(own_any.at[0], label_ref.at[0], sems.at[0]).start()
        pltpu.make_async_copy(other_any.at[0], label_ref.at[1], sems.at[1]).start()

    @pl.when(mine != 0)
    def _():
        pltpu.make_async_copy(other_any.at[0], label_ref.at[0], sems.at[0]).start()
        pltpu.make_async_copy(own_any.at[0], label_ref.at[1], sems.at[1]).start()

    for section in range(2):
        set_matrix(matrix_ref, section, factor_ref)
    line_solve(0, back_ref, small_ref, line_ref, edge_ref, matrix_ref, row_ref, 2 * pairs)
    pltpu.make_async_copy(own_any.at[0], label_ref.at[0], sems.at[0]).wait()
    pltpu.make_async_copy(own_any.at[0], label_ref.at[1], sems.at[1]).wait()

    def enter(pair, _):
        take_in(0, pair, value_in, label_ref.at[0], back_ref, column_ref, row_ref, operand_ref)
        row_pass(0, operand_ref, factor_ref, grid_ref, edge_ref, pair)
        return 0

    lax.fori_loop(0, pairs, enter, 0)
    scan_rows(edge_ref, carry_ref, row_ref, 0, pairs)

    def turn(pair, _):
        value_ref[...] = column_pass(0, operand_ref, factor_ref, column_ref, carry_ref, grid_ref, pair)[0:264]
        for half in range(2):
            block = 2 * pair + half
            inner = slice(128 * half, 128 * half + 128)
            lanes = lanes_of(pair, half)
            left, right = line_at(line_ref, block)
            for top in range(0, BLOCK, CHUNK):
                rows = slice(top, top + CHUNK)
                value = (value_ref[rows, inner], value_ref[top + 128 : top + 128 + CHUNK, inner])
                value = add_reach(column_ref, 0, rows, value, left, right)
                labels = label_ref[1, rows, lanes]
                value = c_mul((pick(row_ref, 1, 0, labels), pick(row_ref, 1, 1, labels)), value)
                zones = zone_ref[rows, lanes]
                value = c_mul((pick(row_ref, 1, 2, zones), pick(row_ref, 1, 3, zones)), value)
                put_operand(operand_ref, 128 * half + top, *value)
        row_pass(1, operand_ref, factor_ref, grid_ref, edge_ref, pair)
        return 0

    lax.fori_loop(0, pairs, turn, 0)
    scan_rows(edge_ref, carry_ref, row_ref, 1, pairs)

    def leave(pair, _):
        value = column_pass(1, operand_ref, factor_ref, column_ref, carry_ref, grid_ref, pair)
        value_ref[...] = value[0:264]
        wide = pl.ds(pl.multiple_of(256 * pair, 256), 256)
        out_ref[0, :, wide] = value[0:128]
        out_ref[1, :, wide] = value[128:256]
        pack_sums(1, value_ref, lambda half, rows: label_ref[1, rows, lanes_of(pair, half)], pair, row_ref, column_ref,
                  value_ref[256:264, :], sums_ref)
        return 0

    lax.fori_loop(0, pairs, leave, 0)


def third_kernel(pairs, value_in, back_ref, own_any, other_any, matrix_ref, column_ref, row_ref, out_ref,
                 label_ref, factor_ref, operand_ref, grid_ref, edge_ref, carry_ref, value_ref, small_ref, line_ref, sems):
    mine = lax.axis_index("sect")

    @pl.when(mine == 0)
    def _():
        pltpu.make_async_copy(other_any.at[0], label_ref, sems.at[0]).start()

    @pl.when(mine != 0)
    def _():
        pltpu.make_async_copy(own_any.at[0], label_ref, sems.at[0]).start()

    set_matrix(matrix_ref, 1, factor_ref)
    line_solve(1, back_ref, small_ref, line_ref, edge_ref, matrix_ref, row_ref, 2 * pairs)
    pltpu.make_async_copy(own_any.at[0], label_ref, sems.at[0]).wait()

    def enter(pair, _):
        take_in(1, pair, value_in, label_ref, back_ref, column_ref, row_ref, operand_ref)
        row_pass(1, operand_ref, factor_ref, grid_ref, edge_ref, pair)
        return 0

    lax.fori_loop(0, pairs, enter, 0)
    scan_rows(edge_ref, carry_ref, row_ref, 1, pairs)

    def leave(pair, _):
        value_ref[...] = column_pass(1, operand_ref, factor_ref, column_ref, carry_ref, grid_ref, pair)[0:264]
        for half in range(2):
            block = 2 * pair + half
            inner = slice(128 * half, 128 * half + 128)
            lanes = lanes_of(pair, half)
            left, right = line_at(line_ref, block)
            for top in range(0, BLOCK, CHUNK):
                rows = slice(top, top + CHUNK)
                value = (value_ref[rows, inner], value_ref[top + 128 : top + 128 + CHUNK, inner])
                value = add_reach(column_ref, 1, rows, value, left, right)
                out_ref[0, 0, rows, lanes] = value[0]
                out_ref[0, 1, rows, lanes] = value[1]
        return 0

    lax.fori_loop(0, pairs, leave, 0)


ANY = pl.BlockSpec(memory_space=pl.ANY)
VMEM = pl.BlockSpec(memory_space=pltpu.VMEM)
SMEM = pl.BlockSpec(memory_space=pltpu.SMEM)


def call(body, in_specs, out_shape, scratch=()):
    out_specs = jax.tree.map(lambda _: VMEM, out_shape)
    return pl.pallas_call(
        body,
        in_specs=in_specs,
        out_specs=out_specs,
        out_shape=out_shape,
        scratch_shapes=list(scratch),
        compiler_params=pltpu.CompilerParams(vmem_limit_bytes=VMEM_LIMIT),
        interpret=INTERPRET,
    )


def fast_shards(fields, region_ids, index_offsets, step_lengths, wave_numbers, zone_ids, zone_phases):
    peers = lax.axis_size("slab")
    width = fields.shape[-1]
    pairs = width // 256
    other = lax.ppermute(region_ids, "sect", [(0, 1), (1, 0)])

    def shape(*sizes):
        return jax.ShapeDtypeStruct(sizes, F32)

    def padded(table):
        return jnp.pad(table, ((0, 0), (0, BLOCK - table.shape[1])))

    matrix, column, row = call(
        partial(prepare_kernel, width),
        [SMEM, SMEM, VMEM, VMEM],
        (shape(2, 384, 256), shape(2, 12, BLOCK, BLOCK), shape(2, 8 * 14, BLOCK)),
    )(wave_numbers, step_lengths, padded(index_offsets), padded(zone_phases))
    solve = [
        pltpu.VMEM((2, LHS_ROWS, 768), BF16),
        pltpu.VMEM((256, 512), BF16),
        pltpu.VMEM((pairs, 256, 256), F32),
        pltpu.VMEM((pairs, 8, 256), F32),
        pltpu.VMEM((2 * pairs, 8, BLOCK), F32),
        pltpu.VMEM((264, 256), F32),
    ]
    small = [pltpu.VMEM((16 * pairs, 256), F32), pltpu.VMEM((16 * pairs, 384), F32)]
    labels = pltpu.VMEM((BLOCK, width), jnp.int32)
    sems = pltpu.SemaphoreType.DMA((2,))
    grids = (shape(2, BLOCK, width), shape(peers, 16, BLOCK))

    def exchange(sums, section):
        held = lax.all_to_all(sums, "slab", 0, 0, tiled=True)
        back = call(partial(middle_kernel, peers, section), [VMEM, VMEM], shape(peers, 8, BLOCK))(held, row)
        return lax.all_to_all(back, "slab", 0, 0, tiled=True)

    value, sums = call(
        partial(first_kernel, pairs), [ANY, ANY, ANY, VMEM, VMEM, VMEM], grids,
        [pltpu.VMEM((2, BLOCK, width), F32), labels] + solve + [sems],
    )(fields, region_ids, other, matrix, column, row)
    back = exchange(sums, 0)
    value, sums = call(
        partial(second_kernel, pairs), [VMEM, VMEM, ANY, ANY, VMEM, VMEM, VMEM, VMEM], grids,
        [pltpu.VMEM((2, BLOCK, width), jnp.int32)] + solve + small + [sems],
    )(value, back, region_ids, other, zone_ids, matrix, column, row)
    back = exchange(sums, 1)
    return call(
        partial(third_kernel, pairs), [VMEM, VMEM, ANY, ANY, VMEM, VMEM, VMEM], shape(1, 2, BLOCK, width),
        [labels] + solve + small + [sems],
    )(value, back, region_ids, other, matrix, column, row)


def choose(fields, *others):
    rows, width = fields.shape[-2:]
    if rows == BLOCK and width == BLOCK * lax.axis_size("slab") and lax.axis_size("sect") == 2:
        return fast_shards(fields, *others)
    return shards(fields, *others)


def solution(mesh):
    return jax.shard_map(
        choose,
        mesh=mesh,
        in_specs=(
            P(None, None, "slab", None),
            P("sect", "slab", None),
            P(),
            P(),
            P(),
            P("slab", None),
            P(),
        ),
        out_specs=P("sect", None, "slab", None),
        check_vma=False,
    )
```

```python
from functools import partial

import jax
import jax.numpy as jnp
from jax import lax
from jax.experimental import pallas as pl
from jax.experimental.pallas import tpu as pltpu
from jax.sharding import PartitionSpec as P

STEPS = 2
BLOCK = 128
INTERPRET = False
HIGHEST = lax.Precision.HIGHEST


def c_mul(a, b):
    return a[0] * b[0] - a[1] * b[1], a[0] * b[1] + a[1] * b[0]


def c_add(a, b):
    return a[0] + b[0], a[1] + b[1]


def c_div(a, b):
    size = b[0] * b[0] + b[1] * b[1]
    return (a[0] * b[0] + a[1] * b[1]) / size, (a[1] * b[0] - a[0] * b[1]) / size


def c_sqrt(a):
    size = jnp.sqrt(a[0] * a[0] + a[1] * a[1])
    real = jnp.sqrt(0.5 * (size + a[0]))
    return real, 0.5 * a[1] / real


def c_power(theta, count):
    size = jnp.exp(-theta[0] * count)
    angle = theta[1] * count
    return size * jnp.cos(angle), -size * jnp.sin(angle)


def scalars(number, length):
    sigma = number * length * 0.25
    size = 0.0625 + sigma * sigma
    square = number * number / size
    z = (-0.0625 * square, -0.25 * sigma * square)
    sinh = c_sqrt(z)
    cosh = c_sqrt((1.0 + z[0], z[1]))
    small = c_add(sinh, c_div(z, (1.0 + cosh[0], cosh[1])))
    theta = (
        jnp.log1p(2.0 * small[0] + small[0] * small[0] + small[1] * small[1]),
        2.0 * jnp.arctan2(small[1], 1.0 + small[0]),
    )
    front = (-2.0 * sigma * sigma / size, -0.5 * sigma / size)
    gamma = c_mul(front, c_div(sinh, cosh))
    alpha = ((0.0625 - sigma * sigma) / size, 0.5 * sigma / size)
    return theta, gamma, c_mul(alpha, alpha)


def closure(theta, total):
    power = c_power(theta, float(total))
    return c_div((jnp.ones_like(power[0]), jnp.zeros_like(power[0])), (1.0 - power[0], -power[1]))


def toeplitz(theta, gamma, count):
    index = jnp.arange(count, dtype=jnp.int32)
    apart = jnp.abs(index[:, None] - index[None, :])
    real, imaginary = c_mul(gamma, c_power(theta, apart.astype(jnp.float32)))
    return jnp.where(apart == 0, 1.0, 0.0) + real, imaginary


def circulant(theta, size, blocks):
    index = jnp.arange(blocks, dtype=jnp.int32)
    apart = jnp.mod(index[:, None] - index[None, :] - 1, blocks).astype(jnp.float32)
    return c_mul(closure(theta, size * blocks), c_power(theta, apart * size))


def c_ein(spec, a, b):
    def one(x, y):
        return jnp.einsum(spec, x, y, precision=HIGHEST)

    return one(a[0], b[0]) - one(a[1], b[1]), one(a[0], b[1]) + one(a[1], b[0])


def spans(theta, gamma, count):
    index = jnp.arange(count, dtype=jnp.int32).astype(jnp.float32)
    weight_left = c_mul(gamma, c_power(theta, count - 1 - index))
    weight_right = c_mul(gamma, c_power(theta, index))
    reach_left = c_power(theta, index + 1)
    reach_right = c_power(theta, count - index)
    return weight_left, weight_right, reach_left, reach_right


def row_solve(x, theta, gamma):
    shape = x[0].shape
    blocks = shape[-1] // BLOCK
    x = tuple(part.reshape(shape[:-1] + (blocks, BLOCK)) for part in x)
    weight_left, weight_right, reach_left, reach_right = spans(theta, gamma, BLOCK)
    ring = circulant(theta, BLOCK, blocks)
    y = c_ein("...bi,ij->...bj", x, toeplitz(theta, gamma, BLOCK))
    left = c_ein("...b,cb->...c", c_ein("...bi,i->...b", x, weight_left), ring)
    right = c_ein("...b,bc->...c", c_ein("...bi,i->...b", x, weight_right), ring)
    y = c_add(y, c_ein("...b,i->...bi", left, reach_left))
    y = c_add(y, c_ein("...b,i->...bi", right, reach_right))
    return tuple(part.reshape(shape) for part in y)


def pick_values(labels, table):
    picked = jnp.zeros(labels.shape, jnp.float32)
    for entry in range(table.shape[-1]):
        picked = picked + jnp.where(labels == entry, table[entry], 0.0)
    return picked


def column_local(x, theta, gamma, rows):
    weight_left, weight_right, _, _ = spans(theta, gamma, rows)
    y = c_ein("ij,jm->im", toeplitz(theta, gamma, rows), x)
    return y, c_ein("i,im->m", weight_left, x), c_ein("i,im->m", weight_right, x)


def reach(y, left, right, theta, gamma, rows):
    _, _, reach_left, reach_right = spans(theta, gamma, rows)
    y = c_add(y, c_ein("i,m->im", reach_left, left))
    return c_add(y, c_ein("i,m->im", reach_right, right))


def payload(y, left, right, screen, theta, gamma, rows):
    weight_left, weight_right, reach_left, reach_right = spans(theta, gamma, rows)
    z = c_mul(screen, y)
    parts = [left, right, c_ein("i,im->m", weight_left, z), c_ein("i,im->m", weight_right, z)]
    for weight, other in ((weight_left, reach_left), (weight_left, reach_right), (weight_right, reach_left)):
        parts.append(c_ein("i,im->m", c_mul(weight, other), screen))
    return jnp.stack([half for part in parts for half in part])


def exchange(packed, theta, rows):
    peers = lax.axis_size("slab")
    width = packed.shape[-1] // peers
    sent = jnp.swapaxes(packed.reshape(packed.shape[0], peers, width), 0, 1)
    held = lax.all_to_all(sent, "slab", 0, 0, tiled=True)
    one = [(held[:, 2 * i], held[:, 2 * i + 1]) for i in range(7)]
    ring = circulant(theta, rows, peers)
    left = c_ein("cb,bm->cm", ring, one[0])
    right = c_ein("bc,bm->cm", ring, one[1])
    next_left = c_add(one[2], c_add(c_mul(one[4], left), c_mul(one[5], right)))
    next_right = c_add(one[3], c_add(c_mul(one[6], left), c_mul(one[4], right)))
    next_left = c_ein("cb,bm->cm", ring, next_left)
    next_right = c_ein("bc,bm->cm", ring, next_right)
    back = jnp.stack([half for part in (left, right, next_left, next_right) for half in part], axis=1)
    back = lax.all_to_all(back, "slab", 0, 0, tiled=True)
    back = jnp.swapaxes(back, 0, 1).reshape(8, peers * width)
    return [(back[2 * i], back[2 * i + 1]) for i in range(4)]


def shards(fields, region_ids, index_offsets, step_lengths, wave_numbers, zone_ids, zone_phases):
    mine = lax.axis_index("sect")
    other = lax.ppermute(region_ids, "sect", [(0, 1), (1, 0)])
    labels = [jnp.where(mine == s, region_ids[0], other[0]) for s in range(2)]
    field = lax.dynamic_index_in_dim(fields, mine, 0, False)
    number = lax.dynamic_index_in_dim(wave_numbers, mine, 0, False)
    phases = lax.dynamic_index_in_dim(zone_phases, mine, 0, False)
    rows = field.shape[1]
    u = (field[0], field[1])
    lens = (pick_values(zone_ids, jnp.cos(phases)), pick_values(zone_ids, jnp.sin(phases)))
    for section in range(2):
        theta, gamma, turn = scalars(number, step_lengths[section])
        phase = number * step_lengths[section] * index_offsets[section]
        table = c_mul(turn, (jnp.cos(phase), jnp.sin(phase)))
        screen = tuple(pick_values(labels[section], half) for half in table)
        u = c_mul(u, screen)
        if section == 1:
            u = c_mul(u, lens)
        u, left, right = column_local(row_solve(u, theta, gamma), theta, gamma, rows)
        sent = payload(u, left, right, screen, theta, gamma, rows)
        back = exchange(sent, theta, rows)
        u = reach(u, back[0], back[1], theta, gamma, rows)
        u, _, _ = column_local(row_solve(c_mul(u, screen), theta, gamma), theta, gamma, rows)
        left = row_solve(back[2], theta, gamma)
        right = row_solve(back[3], theta, gamma)
        u = reach(u, left, right, theta, gamma, rows)
    return jnp.stack(u)[None]


F32 = jnp.float32
BF16 = jnp.bfloat16
LHS_ROWS = 272
LOADS = 1
SLOTS = 2

CHUNK = 32
VMEM_LIMIT = 22 * 1024 * 1024


def tile_of(value):
    return jnp.full((8, BLOCK), value, F32)


def grid_power(base, exponent, bits):
    real = jnp.ones(exponent.shape, F32)
    imaginary = jnp.zeros(exponent.shape, F32)
    for bit in range(bits):
        on = (exponent // (1 << bit)) % 2 == 1
        step = c_mul((real, imaginary), base)
        real = jnp.where(on, step[0], real)
        imaginary = jnp.where(on, step[1], imaginary)
        base = c_mul(base, base)
    return real, imaginary


def spread_to(pair, shape):
    return tuple(jnp.broadcast_to(part[0:1, 0:1], shape) for part in pair)


def prepare_kernel(total, number_ref, length_ref, offset_ref, zone_ref, factor_ref, weight_ref, row_ref, pad_ref):
    mine = lax.axis_index("sect")
    number = tile_of(number_ref[mine])
    tall = (BLOCK, BLOCK)
    place = lax.broadcasted_iota(jnp.int32, tall, 0)
    across = lax.broadcasted_iota(jnp.int32, tall, 1)
    lane = lax.broadcasted_iota(jnp.int32, (8, BLOCK), 1)
    pad_ref[...] = jnp.zeros((8, BLOCK), F32)
    pad_ref[0:2, 0 : offset_ref.shape[1]] = offset_ref[...]
    pad_ref[2:3, 0 : zone_ref.shape[1]] = zone_ref[pl.ds(mine, 1), :]
    lens = jnp.broadcast_to(pad_ref[2:3, :], (8, BLOCK))
    lens = (jnp.cos(lens), jnp.sin(lens))

    def keep(section, top, bottom, real, imaginary):
        for first, value in ((0, real), (BLOCK, imaginary)):
            high, low = split(value)
            factor_ref[section, top:bottom, first : first + BLOCK] = high
            factor_ref[section, top:bottom, 256 + first : 256 + first + BLOCK] = low
            factor_ref[section, top:bottom, 512 + first : 512 + first + BLOCK] = high

    for section in range(2):
        length = tile_of(length_ref[section])
        sigma = number * length * 0.25
        size = 0.0625 + sigma * sigma
        square = number * number / size
        z = (-0.0625 * square, -0.25 * sigma * square)
        sinh = c_sqrt(z)
        cosh = c_sqrt((1.0 + z[0], z[1]))
        root = (cosh[0] - sinh[0], cosh[1] - sinh[1])
        base = c_mul(root, root)
        gamma = c_mul((-2.0 * sigma * sigma / size, -0.5 * sigma / size), c_div(sinh, cosh))
        alpha = ((0.0625 - sigma * sigma) / size, 0.5 * sigma / size)
        turn = c_mul(alpha, alpha)
        hop = base
        for _ in range(7):
            hop = c_mul(hop, hop)
        whole = hop
        for _ in range(total.bit_length() - 8):
            whole = c_mul(whole, whole)
        close = c_div((jnp.ones_like(whole[0]), jnp.zeros_like(whole[0])), (1.0 - whole[0], -whole[1]))
        wide = spread_to(base, tall)
        gain = spread_to(gamma, tall)
        real, imaginary = c_mul(gain, grid_power(wide, jnp.abs(place - across), 7))
        real = real + jnp.where(place == across, 1.0, 0.0)
        keep(section, 0, 128, real, -imaginary)
        keep(section, 128, 256, imaginary, real)
        ahead = grid_power(base, lane, 7)
        behind = grid_power(base, 127 - lane, 7)
        left = c_mul(gamma, behind)
        right = c_mul(gamma, ahead)
        row = lax.broadcasted_iota(jnp.int32, (16, BLOCK), 0)

        def four(values):
            out = jnp.zeros((16, BLOCK), F32)
            for index, value in enumerate(values):
                out = jnp.where(row == index, jnp.broadcast_to(value[0:1], (16, BLOCK)), out)
            return out

        keep(section, 256, 272, four((left[0], left[1], right[0], right[1])), four((-left[1], left[0], -right[1], right[0])))
        factor_ref[section, 272:384, :] = jnp.zeros((112, 768), BF16)
        phase = number * length * jnp.broadcast_to(pad_ref[section : section + 1, :], (8, BLOCK))
        screen = c_mul(turn, (jnp.cos(phase), jnp.sin(phase)))
        reach_left = c_mul(base, ahead)
        reach_right = c_mul(base, behind)
        both = c_mul(gamma, hop)
        listed = [*screen, *lens, *reach_left, *reach_right, *hop, *close, *both]
        for index, value in enumerate(listed):
            row_ref[section, 8 * index : 8 * index + 8, :] = value
        down = grid_power(wide, place, 7)
        up = grid_power(wide, 127 - place, 7)
        high = c_mul(wide, down)
        low = c_mul(wide, up)
        from_left = c_mul(gain, up)
        from_right = c_mul(gain, down)
        tables = [high, low, from_left, from_right, c_mul(from_left, low), c_mul(from_right, high)]
        for index, table in enumerate(tables):
            weight_ref[section, 2 * index] = table[0]
            weight_ref[section, 2 * index + 1] = table[1]


def split(value):
    high = value.astype(BF16)
    return high, (value - high.astype(F32)).astype(BF16)


def put_operand(operand_ref, top, real, imaginary):
    size = real.shape[0]
    high, low = split(real)
    operand_ref[top : top + size, 0:128] = high
    operand_ref[top : top + size, 256:384] = low
    high, low = split(imaginary)
    operand_ref[top : top + size, 128:256] = high
    operand_ref[top : top + size, 384:512] = low


def multiply(factor_ref, section, operand_ref):
    high = operand_ref[:, 0:256]
    right = jnp.concatenate([high, high, operand_ref[:, 256:512]], axis=1)
    return lax.dot_general(factor_ref[section, 0:LHS_ROWS, :], right, (((1,), (1,)), ((), ())), preferred_element_type=F32)


def add_reach(weight_ref, section, rows, value, line):
    high = (weight_ref[section, 0, rows, :], weight_ref[section, 1, rows, :])
    low = (weight_ref[section, 2, rows, :], weight_ref[section, 3, rows, :])
    return c_add(value, c_add(c_mul(high, (line[0], line[1])), c_mul(low, (line[2], line[3]))))


def line_of(carry_ref, block):
    return [carry_ref[block, part : part + 1, :] for part in range(4)]


def pick(table_ref, section, index, labels):
    table = jnp.broadcast_to(table_ref[section, 8 * index : 8 * index + 1, :], labels.shape)
    return jnp.take_along_axis(table, labels, axis=1, mode="promise_in_bounds")


def screen_at(row_ref, section, labels):
    return pick(row_ref, section, 0, labels), pick(row_ref, section, 1, labels)


def row_line(row_ref, section, index):
    return row_ref[section, 8 * index : 8 * index + 1, :]


def hop_of(row_ref, section):
    return (row_line(row_ref, section, 8), row_line(row_ref, section, 9)), (row_line(row_ref, section, 10), row_line(row_ref, section, 11))


def carries(get, put, count, hop, close):
    for reverse in (False, True):
        order = list(range(count))[:: -1 if reverse else 1]
        total = get(order[0], reverse)
        for index in order[1:]:
            total = c_add(c_mul(hop, total), get(index, reverse))
        carry = c_mul(close, total)
        for index in order:
            put(index, reverse, carry)
            carry = c_add(c_mul(hop, carry), get(index, reverse))


def scan_rows(edge_ref, carry_ref, row_ref, section, pairs):
    hop, close = hop_of(row_ref, section)

    def get(block, reverse):
        first = 2 if reverse else 0
        lanes = slice(128 * (block % 2), 128 * (block % 2) + 128)
        return tuple(edge_ref[block // 2, first + part : first + part + 1, lanes] for part in range(2))

    def put(block, reverse, value):
        for part in range(2):
            first = (2 if reverse else 0) + part
            carry_ref[block, first : first + 1, :] = value[part]

    carries(get, put, 2 * pairs, hop, close)


def row_finish(section, operand_ref, factor_ref, grid_ref, edge_ref, pair):
    out = multiply(factor_ref, section, operand_ref)
    grid_ref[pair] = out[0:256]
    edge_ref[pair] = out[256:264]


def column_stage(section, operand_ref, weight_ref, carry_ref, grid_ref, pair):
    for half in range(2):
        lanes = slice(128 * half, 128 * half + 128)
        line = line_of(carry_ref, 2 * pair + half)
        for top in range(0, BLOCK, CHUNK):
            rows = slice(top, top + CHUNK)
            value = (grid_ref[pair, rows, lanes], grid_ref[pair, top + BLOCK : top + BLOCK + CHUNK, lanes])
            put_operand(operand_ref, 128 * half + top, *add_reach(weight_ref, section, rows, value, line))


def pack_edges(pair, ends, sums_ref):
    for half in range(2):
        sums_ref[2 * pair + half, 0:4, :] = ends[0:4, 128 * half : 128 * half + 128]


def pack_sums(section, out_ref, screen_ref, pair, row_ref, weight_ref, sums_ref):
    for half in range(2):
        block = 2 * pair + half
        lanes = lanes_of(pair, half)
        sums = [jnp.zeros((8, BLOCK), F32) for _ in range(10)]
        for top in range(0, BLOCK, 8):
            rows = slice(top, top + 8)
            screen = (screen_ref[0, rows, lanes], screen_ref[1, rows, lanes])
            value = c_mul(screen, (out_ref[0, rows, lanes], out_ref[1, rows, lanes]))
            weights = [(weight_ref[section, 2 * k, rows, :], weight_ref[section, 2 * k + 1, rows, :]) for k in range(2, 6)]
            terms = (c_mul(weights[0], value), c_mul(weights[1], value), screen, c_mul(weights[2], screen), c_mul(weights[3], screen))
            for k, term in enumerate(terms):
                sums[2 * k] = sums[2 * k] + term[0]
                sums[2 * k + 1] = sums[2 * k + 1] + term[1]
        lines = [jnp.sum(part, axis=0, keepdims=True) for part in sums]
        both = c_mul((row_line(row_ref, section, 12), row_line(row_ref, section, 13)), (lines[4], lines[5]))
        for k, line in enumerate(lines[0:4] + list(both) + lines[6:10]):
            sums_ref[block, 4 + k : 5 + k, :] = line
        sums_ref[block, 14:16, :] = jnp.zeros((2, BLOCK), F32)


def line_solve(section, back_ref, small_ref, line_ref, carry_ref, factor_ref, row_ref, blocks):
    small_ref[...] = jnp.zeros(small_ref.shape, F32)
    for block in range(blocks):
        for side in range(2):
            for part in range(2):
                row = 4 + 2 * side + part
                small_ref[8 * block + side : 8 * block + side + 1, 128 * part : 128 * part + 128] = back_ref[block, row : row + 1, :]
    high, low = split(small_ref[...])
    left = jnp.concatenate([high, high, low], axis=1)
    out = lax.dot_general(left, factor_ref[section], (((1,), (1,)), ((), ())), preferred_element_type=F32)
    line_ref[...] = out
    wide = (8, BLOCK)
    hop, close = (tuple(jnp.broadcast_to(part, wide) for part in pair) for pair in hop_of(row_ref, section))
    reach_left = tuple(row_ref[section, 8 * k : 8 * k + 8, :] for k in (4, 5))
    reach_right = tuple(row_ref[section, 8 * k : 8 * k + 8, :] for k in (6, 7))

    def get(block, reverse):
        first = 258 if reverse else 256
        rows = slice(8 * block, 8 * block + 8)
        return tuple(jnp.broadcast_to(line_ref[rows, first + part : first + part + 1], wide) for part in range(2))

    def put(block, reverse, value):
        rows = slice(8 * block, 8 * block + 8)
        add = c_mul(reach_right if reverse else reach_left, value)
        real = line_ref[rows, 0:128] + add[0]
        imaginary = line_ref[rows, 128:256] + add[1]
        if not reverse:
            line_ref[rows, 0:128] = real
            line_ref[rows, 128:256] = imaginary
        else:
            for side in range(2):
                carry_ref[block, 2 * side : 2 * side + 1, :] = real[side : side + 1]
                carry_ref[block, 2 * side + 1 : 2 * side + 2, :] = imaginary[side : side + 1]

    carries(get, put, blocks, hop, close)


def lanes_of(pair, half):
    return slice(256 * pair + 128 * half, 256 * pair + 128 * half + 128)


def wide_of(pair):
    return slice(256 * pair, 256 * pair + 256)


def steps(count, *bodies):
    for time in range(count + len(bodies) - 1):
        for depth, body in enumerate(bodies):
            if 0 <= time - depth < count:
                body(time - depth)


def first_kernel(pairs, field_any, own_any, other_any, factor_ref, weight_ref, row_ref, out_ref, sums_ref,
                 field_ref, label_ref, screen_ref, operand_ref, grid_ref, edge_ref, carry_ref, sems):
    mine = lax.axis_index("sect")

    def field_copy(pair):
        lanes = wide_of(pair)
        return pltpu.make_async_copy(field_any.at[mine, :, :, lanes], field_ref.at[:, :, lanes], sems.at[0, pair])

    def label_copy(source, pair):
        lanes = wide_of(pair)
        return pltpu.make_async_copy(source.at[0, :, lanes], label_ref.at[:, lanes], sems.at[1, pair])

    @pl.when(mine == 0)
    def _():
        for pair in range(pairs):
            label_copy(own_any, pair).start()
            field_copy(pair).start()

    @pl.when(mine != 0)
    def _():
        for pair in range(pairs):
            label_copy(other_any, pair).start()
            field_copy(pair).start()

    def stage(pair):
        if pair % LOADS == 0:
            for each in range(pair, pair + LOADS):
                field_copy(each).wait()
                label_copy(own_any, each).wait()
        for half in range(2):
            lanes = lanes_of(pair, half)
            for top in range(0, BLOCK, CHUNK):
                rows = slice(top, top + CHUNK)
                screen = screen_at(row_ref, 0, label_ref[rows, lanes])
                screen_ref[0, rows, lanes] = screen[0]
                screen_ref[1, rows, lanes] = screen[1]
                value = c_mul(screen, (field_ref[0, rows, lanes], field_ref[1, rows, lanes]))
                put_operand(operand_ref.at[pair % SLOTS], 128 * half + top, *value)

    steps(pairs, stage, lambda pair: row_finish(0, operand_ref.at[pair % SLOTS], factor_ref, grid_ref, edge_ref, pair))
    scan_rows(edge_ref, carry_ref, row_ref, 0, pairs)

    def leave(pair):
        value = multiply(factor_ref, 0, operand_ref.at[pair % SLOTS])
        out_ref[0, :, wide_of(pair)] = value[0:128]
        out_ref[1, :, wide_of(pair)] = value[128:256]
        pack_edges(pair, value[256:264], sums_ref)

    steps(
        pairs,
        lambda pair: column_stage(0, operand_ref.at[pair % SLOTS], weight_ref, carry_ref, grid_ref, pair),
        leave,
        lambda pair: pack_sums(0, out_ref, screen_ref, pair, row_ref, weight_ref, sums_ref),
    )


def middle_kernel(peers, section, held_ref, row_ref, back_ref):
    hop, close = hop_of(row_ref, section)

    def line(peer, row):
        return held_ref[peer, row : row + 1, :], held_ref[peer, row + 1 : row + 2, :]

    def keep(first):
        def put(peer, reverse, value):
            row = first + (2 if reverse else 0)
            back_ref[peer, row : row + 1, :] = value[0]
            back_ref[peer, row + 1 : row + 2, :] = value[1]

        return put

    carries(lambda peer, reverse: line(peer, 2 if reverse else 0), keep(0), peers, hop, close)

    def later(peer, reverse):
        left = (back_ref[peer, 0:1, :], back_ref[peer, 1:2, :])
        right = (back_ref[peer, 2:3, :], back_ref[peer, 3:4, :])
        if reverse:
            return c_add(line(peer, 6), c_add(c_mul(line(peer, 12), left), c_mul(line(peer, 8), right)))
        return c_add(line(peer, 4), c_add(c_mul(line(peer, 8), left), c_mul(line(peer, 10), right)))

    carries(later, keep(4), peers, hop, close)


def labels_of(section, own_ref, other_ref):
    mine = lax.axis_index("sect")
    return lambda rows, lanes: jnp.where(mine == section, own_ref[0, rows, lanes], other_ref[0, rows, lanes])


def take_in(section, pair, value_in, labels, weight_ref, back_ref, row_ref, operand_ref):
    for half in range(2):
        lanes = lanes_of(pair, half)
        line = line_of(back_ref, 2 * pair + half)
        for top in range(0, BLOCK, CHUNK):
            rows = slice(top, top + CHUNK)
            value = add_reach(weight_ref, section, rows, (value_in[0, rows, lanes], value_in[1, rows, lanes]), line)
            put_operand(operand_ref, 128 * half + top, *c_mul(screen_at(row_ref, section, labels(rows, lanes)), value))


def second_kernel(pairs, value_in, back_ref, own_ref, other_ref, zone_ref, factor_ref, weight_ref, row_ref, out_ref, sums_ref,
                  screen_ref, operand_ref, grid_ref, edge_ref, carry_ref, late_ref, small_ref, line_ref, inner_ref):
    labels = [labels_of(section, own_ref, other_ref) for section in range(2)]
    steps(
        pairs,
        lambda pair: take_in(0, pair, value_in, labels[0], weight_ref, back_ref, row_ref, operand_ref.at[pair % SLOTS]),
        lambda pair: row_finish(0, operand_ref.at[pair % SLOTS], factor_ref, grid_ref, edge_ref, pair),
    )
    line_solve(0, back_ref, small_ref, line_ref, late_ref, factor_ref, row_ref, 2 * pairs)
    scan_rows(edge_ref, carry_ref, row_ref, 0, pairs)

    def turn(pair):
        out = multiply(factor_ref, 0, operand_ref.at[pair % SLOTS])
        for half in range(2):
            inner = slice(128 * half, 128 * half + 128)
            lanes = lanes_of(pair, half)
            line = line_of(late_ref, 2 * pair + half)
            for top in range(0, BLOCK, CHUNK):
                rows = slice(top, top + CHUNK)
                value = (out[rows, inner], out[top + BLOCK : top + BLOCK + CHUNK, inner])
                value = add_reach(weight_ref, 0, rows, value, line)
                screen = screen_at(row_ref, 1, labels[1](rows, lanes))
                screen_ref[0, rows, lanes] = screen[0]
                screen_ref[1, rows, lanes] = screen[1]
                zones = zone_ref[rows, lanes]
                value = c_mul((pick(row_ref, 1, 2, zones), pick(row_ref, 1, 3, zones)), c_mul(screen, value))
                put_operand(inner_ref.at[pair % SLOTS], 128 * half + top, *value)

    steps(
        pairs,
        lambda pair: column_stage(0, operand_ref.at[pair % SLOTS], weight_ref, carry_ref, grid_ref, pair),
        turn,
        lambda pair: row_finish(1, inner_ref.at[pair % SLOTS], factor_ref, grid_ref, edge_ref, pair),
    )
    scan_rows(edge_ref, carry_ref, row_ref, 1, pairs)

    def leave(pair):
        value = multiply(factor_ref, 1, operand_ref.at[pair % SLOTS])
        out_ref[0, :, wide_of(pair)] = value[0:128]
        out_ref[1, :, wide_of(pair)] = value[128:256]
        pack_edges(pair, value[256:264], sums_ref)

    steps(
        pairs,
        lambda pair: column_stage(1, operand_ref.at[pair % SLOTS], weight_ref, carry_ref, grid_ref, pair),
        leave,
        lambda pair: pack_sums(1, out_ref, screen_ref, pair, row_ref, weight_ref, sums_ref),
    )


def third_kernel(pairs, value_in, back_ref, own_ref, other_ref, factor_ref, weight_ref, row_ref, out_ref,
                 operand_ref, grid_ref, edge_ref, carry_ref, late_ref, small_ref, line_ref):
    labels = labels_of(1, own_ref, other_ref)
    steps(
        pairs,
        lambda pair: take_in(1, pair, value_in, labels, weight_ref, back_ref, row_ref, operand_ref.at[pair % SLOTS]),
        lambda pair: row_finish(1, operand_ref.at[pair % SLOTS], factor_ref, grid_ref, edge_ref, pair),
    )
    line_solve(1, back_ref, small_ref, line_ref, late_ref, factor_ref, row_ref, 2 * pairs)
    scan_rows(edge_ref, carry_ref, row_ref, 1, pairs)

    def leave(pair):
        out = multiply(factor_ref, 1, operand_ref.at[pair % SLOTS])
        for half in range(2):
            inner = slice(128 * half, 128 * half + 128)
            lanes = lanes_of(pair, half)
            line = line_of(late_ref, 2 * pair + half)
            for top in range(0, BLOCK, CHUNK):
                rows = slice(top, top + CHUNK)
                value = (out[rows, inner], out[top + BLOCK : top + BLOCK + CHUNK, inner])
                value = add_reach(weight_ref, 1, rows, value, line)
                out_ref[0, 0, rows, lanes] = value[0]
                out_ref[0, 1, rows, lanes] = value[1]

    steps(pairs, lambda pair: column_stage(1, operand_ref.at[pair % SLOTS], weight_ref, carry_ref, grid_ref, pair), leave)


ANY = pl.BlockSpec(memory_space=pl.ANY)
VMEM = pl.BlockSpec(memory_space=pltpu.VMEM)
SMEM = pl.BlockSpec(memory_space=pltpu.SMEM)


def call(body, in_specs, out_shape, scratch=()):
    out_specs = jax.tree.map(lambda _: VMEM, out_shape)
    return pl.pallas_call(
        body,
        in_specs=in_specs,
        out_specs=out_specs,
        out_shape=out_shape,
        scratch_shapes=list(scratch),
        compiler_params=pltpu.CompilerParams(vmem_limit_bytes=VMEM_LIMIT),
        interpret=INTERPRET,
    )


def shape(*sizes, kind=F32):
    return jax.ShapeDtypeStruct(sizes, kind)


def kernels(peers, width):
    pairs = width // 256
    passing = [
        pltpu.VMEM((SLOTS, 256, 512), BF16),
        pltpu.VMEM((pairs, 256, 256), F32),
        pltpu.VMEM((pairs, 8, 256), F32),
        pltpu.VMEM((2 * pairs, 8, BLOCK), F32),
    ]
    small = [pltpu.VMEM((2 * pairs, 8, BLOCK), F32), pltpu.VMEM((16 * pairs, 256), F32), pltpu.VMEM((16 * pairs, 384), F32)]
    screen = pltpu.VMEM((2, BLOCK, width), F32)
    grids = (shape(2, BLOCK, width), shape(peers, 16, BLOCK))
    prepare = call(
        partial(prepare_kernel, width),
        [SMEM, SMEM, VMEM, VMEM],
        (shape(2, 384, 768, kind=BF16), shape(2, 12, BLOCK, BLOCK), shape(2, 8 * 14, BLOCK)),
        [pltpu.VMEM((8, BLOCK), F32)],
    )
    first = call(
        partial(first_kernel, pairs), [ANY] * 3 + [VMEM] * 3, grids,
        [pltpu.VMEM((2, BLOCK, width), F32), pltpu.VMEM((BLOCK, width), jnp.int32), screen]
        + passing
        + [pltpu.SemaphoreType.DMA((2, pairs))],
    )
    middle = [call(partial(middle_kernel, peers, section), [VMEM, VMEM], shape(peers, 8, BLOCK)) for section in range(2)]
    second = call(partial(second_kernel, pairs), [VMEM] * 8, grids, [screen] + passing + small + passing[:1])
    third = call(partial(third_kernel, pairs), [VMEM] * 7, shape(1, 2, BLOCK, width), passing + small)
    return prepare, first, middle, second, third


def stay(value):
    return value if INTERPRET else pltpu.with_memory_space_constraint(value, pltpu.HBM)


def fast_shards(fields, region_ids, index_offsets, step_lengths, wave_numbers, zone_ids, zone_phases):
    prepare, first, middle, second, third = kernels(lax.axis_size("slab"), fields.shape[-1])
    other = lax.ppermute(region_ids, "sect", [(0, 1), (1, 0)])
    factor, weights, row = prepare(stay(wave_numbers), stay(step_lengths), stay(index_offsets), stay(zone_phases))

    def exchange(sums, section):
        held = lax.all_to_all(sums, "slab", 0, 0, tiled=True)
        return lax.all_to_all(middle[section](held, row), "slab", 0, 0, tiled=True)

    value, sums = first(stay(fields), stay(region_ids), other, factor, weights, row)
    back = exchange(sums, 0)
    value, sums = second(value, back, region_ids, other, zone_ids, factor, weights, row)
    back = exchange(sums, 1)
    return third(value, back, region_ids, other, factor, weights, row)


def choose(fields, *others):
    rows, width = fields.shape[-2:]
    if rows == BLOCK and width == BLOCK * lax.axis_size("slab") and lax.axis_size("sect") == 2:
        return fast_shards(fields, *others)
    return shards(fields, *others)


def solution(mesh):
    return jax.shard_map(
        choose,
        mesh=mesh,
        in_specs=(
            P(None, None, "slab", None),
            P("sect", "slab", None),
            P(),
            P(),
            P(),
            P("slab", None),
            P(),
        ),
        out_specs=P("sect", None, "slab", None),
        check_vma=False,
    )
```

```python
from functools import partial

import jax
import jax.numpy as jnp
from jax import lax
from jax.experimental import pallas as pl
from jax.experimental.pallas import tpu as pltpu
from jax.sharding import PartitionSpec as P

STEPS = 2
BLOCK = 128
INTERPRET = False
HIGHEST = lax.Precision.HIGHEST


def c_mul(a, b):
    return a[0] * b[0] - a[1] * b[1], a[0] * b[1] + a[1] * b[0]


def c_add(a, b):
    return a[0] + b[0], a[1] + b[1]


def c_div(a, b):
    size = b[0] * b[0] + b[1] * b[1]
    return (a[0] * b[0] + a[1] * b[1]) / size, (a[1] * b[0] - a[0] * b[1]) / size


def c_sqrt(a):
    size = jnp.sqrt(a[0] * a[0] + a[1] * a[1])
    real = jnp.sqrt(0.5 * (size + a[0]))
    return real, 0.5 * a[1] / real


def c_power(theta, count):
    size = jnp.exp(-theta[0] * count)
    angle = theta[1] * count
    return size * jnp.cos(angle), -size * jnp.sin(angle)


def scalars(number, length):
    sigma = number * length * 0.25
    size = 0.0625 + sigma * sigma
    square = number * number / size
    z = (-0.0625 * square, -0.25 * sigma * square)
    sinh = c_sqrt(z)
    cosh = c_sqrt((1.0 + z[0], z[1]))
    small = c_add(sinh, c_div(z, (1.0 + cosh[0], cosh[1])))
    theta = (
        jnp.log1p(2.0 * small[0] + small[0] * small[0] + small[1] * small[1]),
        2.0 * jnp.arctan2(small[1], 1.0 + small[0]),
    )
    front = (-2.0 * sigma * sigma / size, -0.5 * sigma / size)
    gamma = c_mul(front, c_div(sinh, cosh))
    alpha = ((0.0625 - sigma * sigma) / size, 0.5 * sigma / size)
    return theta, gamma, c_mul(alpha, alpha)


def closure(theta, total):
    power = c_power(theta, float(total))
    return c_div((jnp.ones_like(power[0]), jnp.zeros_like(power[0])), (1.0 - power[0], -power[1]))


def toeplitz(theta, gamma, count):
    index = jnp.arange(count, dtype=jnp.int32)
    apart = jnp.abs(index[:, None] - index[None, :])
    real, imaginary = c_mul(gamma, c_power(theta, apart.astype(jnp.float32)))
    return jnp.where(apart == 0, 1.0, 0.0) + real, imaginary


def circulant(theta, size, blocks):
    index = jnp.arange(blocks, dtype=jnp.int32)
    apart = jnp.mod(index[:, None] - index[None, :] - 1, blocks).astype(jnp.float32)
    return c_mul(closure(theta, size * blocks), c_power(theta, apart * size))


def c_ein(spec, a, b):
    def one(x, y):
        return jnp.einsum(spec, x, y, precision=HIGHEST)

    return one(a[0], b[0]) - one(a[1], b[1]), one(a[0], b[1]) + one(a[1], b[0])


def spans(theta, gamma, count):
    index = jnp.arange(count, dtype=jnp.int32).astype(jnp.float32)
    weight_left = c_mul(gamma, c_power(theta, count - 1 - index))
    weight_right = c_mul(gamma, c_power(theta, index))
    reach_left = c_power(theta, index + 1)
    reach_right = c_power(theta, count - index)
    return weight_left, weight_right, reach_left, reach_right


def row_solve(x, theta, gamma):
    shape = x[0].shape
    blocks = shape[-1] // BLOCK
    x = tuple(part.reshape(shape[:-1] + (blocks, BLOCK)) for part in x)
    weight_left, weight_right, reach_left, reach_right = spans(theta, gamma, BLOCK)
    ring = circulant(theta, BLOCK, blocks)
    y = c_ein("...bi,ij->...bj", x, toeplitz(theta, gamma, BLOCK))
    left = c_ein("...b,cb->...c", c_ein("...bi,i->...b", x, weight_left), ring)
    right = c_ein("...b,bc->...c", c_ein("...bi,i->...b", x, weight_right), ring)
    y = c_add(y, c_ein("...b,i->...bi", left, reach_left))
    y = c_add(y, c_ein("...b,i->...bi", right, reach_right))
    return tuple(part.reshape(shape) for part in y)


def pick_values(labels, table):
    picked = jnp.zeros(labels.shape, jnp.float32)
    for entry in range(table.shape[-1]):
        picked = picked + jnp.where(labels == entry, table[entry], 0.0)
    return picked


def column_local(x, theta, gamma, rows):
    weight_left, weight_right, _, _ = spans(theta, gamma, rows)
    y = c_ein("ij,jm->im", toeplitz(theta, gamma, rows), x)
    return y, c_ein("i,im->m", weight_left, x), c_ein("i,im->m", weight_right, x)


def reach(y, left, right, theta, gamma, rows):
    _, _, reach_left, reach_right = spans(theta, gamma, rows)
    y = c_add(y, c_ein("i,m->im", reach_left, left))
    return c_add(y, c_ein("i,m->im", reach_right, right))


def payload(y, left, right, screen, theta, gamma, rows):
    weight_left, weight_right, reach_left, reach_right = spans(theta, gamma, rows)
    z = c_mul(screen, y)
    parts = [left, right, c_ein("i,im->m", weight_left, z), c_ein("i,im->m", weight_right, z)]
    for weight, other in ((weight_left, reach_left), (weight_left, reach_right), (weight_right, reach_left)):
        parts.append(c_ein("i,im->m", c_mul(weight, other), screen))
    return jnp.stack([half for part in parts for half in part])


def exchange(packed, theta, rows):
    peers = lax.axis_size("slab")
    width = packed.shape[-1] // peers
    sent = jnp.swapaxes(packed.reshape(packed.shape[0], peers, width), 0, 1)
    held = lax.all_to_all(sent, "slab", 0, 0, tiled=True)
    one = [(held[:, 2 * i], held[:, 2 * i + 1]) for i in range(7)]
    ring = circulant(theta, rows, peers)
    left = c_ein("cb,bm->cm", ring, one[0])
    right = c_ein("bc,bm->cm", ring, one[1])
    next_left = c_add(one[2], c_add(c_mul(one[4], left), c_mul(one[5], right)))
    next_right = c_add(one[3], c_add(c_mul(one[6], left), c_mul(one[4], right)))
    next_left = c_ein("cb,bm->cm", ring, next_left)
    next_right = c_ein("bc,bm->cm", ring, next_right)
    back = jnp.stack([half for part in (left, right, next_left, next_right) for half in part], axis=1)
    back = lax.all_to_all(back, "slab", 0, 0, tiled=True)
    back = jnp.swapaxes(back, 0, 1).reshape(8, peers * width)
    return [(back[2 * i], back[2 * i + 1]) for i in range(4)]


def shards(fields, region_ids, index_offsets, step_lengths, wave_numbers, zone_ids, zone_phases):
    mine = lax.axis_index("sect")
    other = lax.ppermute(region_ids, "sect", [(0, 1), (1, 0)])
    labels = [jnp.where(mine == s, region_ids[0], other[0]) for s in range(2)]
    field = lax.dynamic_index_in_dim(fields, mine, 0, False)
    number = lax.dynamic_index_in_dim(wave_numbers, mine, 0, False)
    phases = lax.dynamic_index_in_dim(zone_phases, mine, 0, False)
    rows = field.shape[1]
    u = (field[0], field[1])
    lens = (pick_values(zone_ids, jnp.cos(phases)), pick_values(zone_ids, jnp.sin(phases)))
    for section in range(2):
        theta, gamma, turn = scalars(number, step_lengths[section])
        phase = number * step_lengths[section] * index_offsets[section]
        table = c_mul(turn, (jnp.cos(phase), jnp.sin(phase)))
        screen = tuple(pick_values(labels[section], half) for half in table)
        u = c_mul(u, screen)
        if section == 1:
            u = c_mul(u, lens)
        u, left, right = column_local(row_solve(u, theta, gamma), theta, gamma, rows)
        sent = payload(u, left, right, screen, theta, gamma, rows)
        back = exchange(sent, theta, rows)
        u = reach(u, back[0], back[1], theta, gamma, rows)
        u, _, _ = column_local(row_solve(c_mul(u, screen), theta, gamma), theta, gamma, rows)
        left = row_solve(back[2], theta, gamma)
        right = row_solve(back[3], theta, gamma)
        u = reach(u, left, right, theta, gamma, rows)
    return jnp.stack(u)[None]


F32 = jnp.float32
BF16 = jnp.bfloat16
LHS_ROWS = 272
SLOTS = 2

CHUNK = 32
VMEM_LIMIT = 22 * 1024 * 1024


def tile_of(value):
    return jnp.full((8, BLOCK), value, F32)


def grid_power(base, exponent, bits):
    real = jnp.ones(exponent.shape, F32)
    imaginary = jnp.zeros(exponent.shape, F32)
    for bit in range(bits):
        on = (exponent // (1 << bit)) % 2 == 1
        step = c_mul((real, imaginary), base)
        real = jnp.where(on, step[0], real)
        imaginary = jnp.where(on, step[1], imaginary)
        base = c_mul(base, base)
    return real, imaginary


def spread_to(pair, shape):
    return tuple(jnp.broadcast_to(part[0:1, 0:1], shape) for part in pair)


def prepare_kernel(total, number_ref, length_ref, offset_ref, zone_ref, field_any, label_any,
                   factor_ref, weight_ref, row_ref, field_ref, label_ref, pad_ref, sems):
    mine = lax.axis_index("sect")
    copies = [
        pltpu.make_async_copy(field_any.at[mine], field_ref, sems.at[0]),
        pltpu.make_async_copy(label_any, label_ref, sems.at[1]),
    ]
    for copy in copies:
        copy.start()
    number = tile_of(number_ref[mine])
    tall = (BLOCK, BLOCK)
    place = lax.broadcasted_iota(jnp.int32, tall, 0)
    across = lax.broadcasted_iota(jnp.int32, tall, 1)
    lane = lax.broadcasted_iota(jnp.int32, (8, BLOCK), 1)
    pad_ref[...] = jnp.zeros((8, BLOCK), F32)
    pad_ref[0:2, 0 : offset_ref.shape[1]] = offset_ref[...]
    pad_ref[2:3, 0 : zone_ref.shape[1]] = zone_ref[pl.ds(mine, 1), :]
    lens = jnp.broadcast_to(pad_ref[2:3, :], (8, BLOCK))
    lens = (jnp.cos(lens), jnp.sin(lens))

    def keep(section, top, bottom, real, imaginary):
        for first, value in ((0, real), (BLOCK, imaginary)):
            high, low = split(value)
            factor_ref[section, top:bottom, first : first + BLOCK] = high
            factor_ref[section, top:bottom, 256 + first : 256 + first + BLOCK] = low
            factor_ref[section, top:bottom, 512 + first : 512 + first + BLOCK] = high

    for section in range(2):
        length = tile_of(length_ref[section])
        sigma = number * length * 0.25
        size = 0.0625 + sigma * sigma
        square = number * number / size
        z = (-0.0625 * square, -0.25 * sigma * square)
        sinh = c_sqrt(z)
        cosh = c_sqrt((1.0 + z[0], z[1]))
        root = (cosh[0] - sinh[0], cosh[1] - sinh[1])
        base = c_mul(root, root)
        gamma = c_mul((-2.0 * sigma * sigma / size, -0.5 * sigma / size), c_div(sinh, cosh))
        alpha = ((0.0625 - sigma * sigma) / size, 0.5 * sigma / size)
        turn = c_mul(alpha, alpha)
        hop = base
        for _ in range(7):
            hop = c_mul(hop, hop)
        whole = hop
        for _ in range(total.bit_length() - 8):
            whole = c_mul(whole, whole)
        close = c_div((jnp.ones_like(whole[0]), jnp.zeros_like(whole[0])), (1.0 - whole[0], -whole[1]))
        wide = spread_to(base, tall)
        gain = spread_to(gamma, tall)
        real, imaginary = c_mul(gain, grid_power(wide, jnp.abs(place - across), 7))
        real = real + jnp.where(place == across, 1.0, 0.0)
        keep(section, 0, 128, real, -imaginary)
        keep(section, 128, 256, imaginary, real)
        ahead = grid_power(base, lane, 7)
        behind = grid_power(base, 127 - lane, 7)
        left = c_mul(gamma, behind)
        right = c_mul(gamma, ahead)
        row = lax.broadcasted_iota(jnp.int32, (16, BLOCK), 0)

        def four(values):
            out = jnp.zeros((16, BLOCK), F32)
            for index, value in enumerate(values):
                out = jnp.where(row == index, jnp.broadcast_to(value[0:1], (16, BLOCK)), out)
            return out

        keep(section, 256, 272, four((left[0], left[1], right[0], right[1])), four((-left[1], left[0], -right[1], right[0])))
        factor_ref[section, 272:384, :] = jnp.zeros((112, 768), BF16)
        phase = number * length * jnp.broadcast_to(pad_ref[section : section + 1, :], (8, BLOCK))
        screen = c_mul(turn, (jnp.cos(phase), jnp.sin(phase)))
        reach_left = c_mul(base, ahead)
        reach_right = c_mul(base, behind)
        both = c_mul(gamma, hop)
        listed = [*screen, *lens, *reach_left, *reach_right, *hop, *close, *both]
        for index, value in enumerate(listed):
            row_ref[section, 8 * index : 8 * index + 8, :] = value
        down = grid_power(wide, place, 7)
        up = grid_power(wide, 127 - place, 7)
        high = c_mul(wide, down)
        low = c_mul(wide, up)
        from_left = c_mul(gain, up)
        from_right = c_mul(gain, down)
        tables = [high, low, from_left, from_right, c_mul(from_left, low), c_mul(from_right, high)]
        for index, table in enumerate(tables):
            weight_ref[section, 2 * index] = table[0]
            weight_ref[section, 2 * index + 1] = table[1]
    for copy in copies:
        copy.wait()


def split(value):
    high = value.astype(BF16)
    return high, (value - high.astype(F32)).astype(BF16)


def put_operand(operand_ref, top, real, imaginary):
    size = real.shape[0]
    high, low = split(real)
    operand_ref[top : top + size, 0:128] = high
    operand_ref[top : top + size, 256:384] = low
    high, low = split(imaginary)
    operand_ref[top : top + size, 128:256] = high
    operand_ref[top : top + size, 384:512] = low


def multiply(factor_ref, section, operand_ref):
    high = operand_ref[:, 0:256]
    right = jnp.concatenate([high, high, operand_ref[:, 256:512]], axis=1)
    return lax.dot_general(factor_ref[section, 0:LHS_ROWS, :], right, (((1,), (1,)), ((), ())), preferred_element_type=F32)


def add_reach(weight_ref, section, rows, value, line):
    high = (weight_ref[section, 0, rows, :], weight_ref[section, 1, rows, :])
    low = (weight_ref[section, 2, rows, :], weight_ref[section, 3, rows, :])
    return c_add(value, c_add(c_mul(high, (line[0], line[1])), c_mul(low, (line[2], line[3]))))


def line_of(carry_ref, block):
    return [carry_ref[block, part : part + 1, :] for part in range(4)]


def pick(table_ref, section, index, labels):
    table = jnp.broadcast_to(table_ref[section, 8 * index : 8 * index + 1, :], labels.shape)
    return jnp.take_along_axis(table, labels, axis=1, mode="promise_in_bounds")


def screen_at(row_ref, section, labels):
    return pick(row_ref, section, 0, labels), pick(row_ref, section, 1, labels)


def row_line(row_ref, section, index):
    return row_ref[section, 8 * index : 8 * index + 1, :]


def hop_of(row_ref, section):
    return (row_line(row_ref, section, 8), row_line(row_ref, section, 9)), (row_line(row_ref, section, 10), row_line(row_ref, section, 11))


def carries(get, put, count, hop, close):
    for reverse in (False, True):
        order = list(range(count))[:: -1 if reverse else 1]
        total = get(order[0], reverse)
        for index in order[1:]:
            total = c_add(c_mul(hop, total), get(index, reverse))
        carry = c_mul(close, total)
        for index in order:
            put(index, reverse, carry)
            carry = c_add(c_mul(hop, carry), get(index, reverse))


def scan_rows(edge_ref, carry_ref, row_ref, section, pairs):
    hop, close = hop_of(row_ref, section)

    def get(block, reverse):
        first = 2 if reverse else 0
        lanes = slice(128 * (block % 2), 128 * (block % 2) + 128)
        return tuple(edge_ref[block // 2, first + part : first + part + 1, lanes] for part in range(2))

    def put(block, reverse, value):
        for part in range(2):
            first = (2 if reverse else 0) + part
            carry_ref[block, first : first + 1, :] = value[part]

    carries(get, put, 2 * pairs, hop, close)


def row_finish(section, operand_ref, factor_ref, grid_ref, edge_ref, pair):
    out = multiply(factor_ref, section, operand_ref)
    grid_ref[pair] = out[0:256]
    edge_ref[pair] = out[256:264]


def column_stage(section, operand_ref, weight_ref, carry_ref, grid_ref, pair):
    for half in range(2):
        lanes = slice(128 * half, 128 * half + 128)
        line = line_of(carry_ref, 2 * pair + half)
        for top in range(0, BLOCK, CHUNK):
            rows = slice(top, top + CHUNK)
            value = (grid_ref[pair, rows, lanes], grid_ref[pair, top + BLOCK : top + BLOCK + CHUNK, lanes])
            put_operand(operand_ref, 128 * half + top, *add_reach(weight_ref, section, rows, value, line))


def pack_edges(pair, ends, sums_ref):
    for half in range(2):
        sums_ref[2 * pair + half, 0:4, :] = ends[0:4, 128 * half : 128 * half + 128]


def pack_sums(section, out_ref, screen_ref, pair, row_ref, weight_ref, sums_ref):
    for half in range(2):
        block = 2 * pair + half
        lanes = lanes_of(pair, half)
        sums = [jnp.zeros((8, BLOCK), F32) for _ in range(10)]
        for top in range(0, BLOCK, 8):
            rows = slice(top, top + 8)
            screen = (screen_ref[0, rows, lanes], screen_ref[1, rows, lanes])
            value = c_mul(screen, (out_ref[0, rows, lanes], out_ref[1, rows, lanes]))
            weights = [(weight_ref[section, 2 * k, rows, :], weight_ref[section, 2 * k + 1, rows, :]) for k in range(2, 6)]
            terms = (c_mul(weights[0], value), c_mul(weights[1], value), screen, c_mul(weights[2], screen), c_mul(weights[3], screen))
            for k, term in enumerate(terms):
                sums[2 * k] = sums[2 * k] + term[0]
                sums[2 * k + 1] = sums[2 * k + 1] + term[1]
        lines = [jnp.sum(part, axis=0, keepdims=True) for part in sums]
        both = c_mul((row_line(row_ref, section, 12), row_line(row_ref, section, 13)), (lines[4], lines[5]))
        for k, line in enumerate(lines[0:4] + list(both) + lines[6:10]):
            sums_ref[block, 4 + k : 5 + k, :] = line
        sums_ref[block, 14:16, :] = jnp.zeros((2, BLOCK), F32)


def line_solve(section, back_ref, small_ref, line_ref, carry_ref, factor_ref, row_ref, blocks):
    small_ref[...] = jnp.zeros(small_ref.shape, F32)
    for block in range(blocks):
        for side in range(2):
            for part in range(2):
                row = 4 + 2 * side + part
                small_ref[8 * block + side : 8 * block + side + 1, 128 * part : 128 * part + 128] = back_ref[block, row : row + 1, :]
    high, low = split(small_ref[...])
    left = jnp.concatenate([high, high, low], axis=1)
    out = lax.dot_general(left, factor_ref[section], (((1,), (1,)), ((), ())), preferred_element_type=F32)
    line_ref[...] = out
    wide = (8, BLOCK)
    hop, close = (tuple(jnp.broadcast_to(part, wide) for part in pair) for pair in hop_of(row_ref, section))
    reach_left = tuple(row_ref[section, 8 * k : 8 * k + 8, :] for k in (4, 5))
    reach_right = tuple(row_ref[section, 8 * k : 8 * k + 8, :] for k in (6, 7))

    def get(block, reverse):
        first = 258 if reverse else 256
        rows = slice(8 * block, 8 * block + 8)
        return tuple(jnp.broadcast_to(line_ref[rows, first + part : first + part + 1], wide) for part in range(2))

    def put(block, reverse, value):
        rows = slice(8 * block, 8 * block + 8)
        add = c_mul(reach_right if reverse else reach_left, value)
        real = line_ref[rows, 0:128] + add[0]
        imaginary = line_ref[rows, 128:256] + add[1]
        if not reverse:
            line_ref[rows, 0:128] = real
            line_ref[rows, 128:256] = imaginary
        else:
            for side in range(2):
                carry_ref[block, 2 * side : 2 * side + 1, :] = real[side : side + 1]
                carry_ref[block, 2 * side + 1 : 2 * side + 2, :] = imaginary[side : side + 1]

    carries(get, put, blocks, hop, close)


def lanes_of(pair, half):
    return slice(256 * pair + 128 * half, 256 * pair + 128 * half + 128)


def wide_of(pair):
    return slice(256 * pair, 256 * pair + 256)


def steps(count, *bodies):
    for time in range(count + len(bodies) - 1):
        for depth, body in enumerate(bodies):
            if 0 <= time - depth < count:
                body(time - depth)


def first_kernel(pairs, field_ref, own_ref, other_ref, factor_ref, weight_ref, row_ref, out_ref, sums_ref, screen_ref,
                 operand_ref, grid_ref, edge_ref, carry_ref):
    labels = labels_of(0, own_ref, other_ref)

    def stage(pair):
        for half in range(2):
            lanes = lanes_of(pair, half)
            for top in range(0, BLOCK, CHUNK):
                rows = slice(top, top + CHUNK)
                screen = screen_at(row_ref, 0, labels(rows, lanes))
                screen_ref[0, rows, lanes] = screen[0]
                screen_ref[1, rows, lanes] = screen[1]
                value = c_mul(screen, (field_ref[0, rows, lanes], field_ref[1, rows, lanes]))
                put_operand(operand_ref.at[pair % SLOTS], 128 * half + top, *value)

    steps(pairs, stage, lambda pair: row_finish(0, operand_ref.at[pair % SLOTS], factor_ref, grid_ref, edge_ref, pair))
    scan_rows(edge_ref, carry_ref, row_ref, 0, pairs)

    def leave(pair):
        value = multiply(factor_ref, 0, operand_ref.at[pair % SLOTS])
        out_ref[0, :, wide_of(pair)] = value[0:128]
        out_ref[1, :, wide_of(pair)] = value[128:256]
        pack_edges(pair, value[256:264], sums_ref)

    steps(
        pairs,
        lambda pair: column_stage(0, operand_ref.at[pair % SLOTS], weight_ref, carry_ref, grid_ref, pair),
        leave,
        lambda pair: pack_sums(0, out_ref, screen_ref, pair, row_ref, weight_ref, sums_ref),
    )


def middle_kernel(peers, section, held_ref, row_ref, back_ref):
    hop, close = hop_of(row_ref, section)

    def line(peer, row):
        return held_ref[peer, row : row + 1, :], held_ref[peer, row + 1 : row + 2, :]

    def keep(first):
        def put(peer, reverse, value):
            row = first + (2 if reverse else 0)
            back_ref[peer, row : row + 1, :] = value[0]
            back_ref[peer, row + 1 : row + 2, :] = value[1]

        return put

    carries(lambda peer, reverse: line(peer, 2 if reverse else 0), keep(0), peers, hop, close)

    def later(peer, reverse):
        left = (back_ref[peer, 0:1, :], back_ref[peer, 1:2, :])
        right = (back_ref[peer, 2:3, :], back_ref[peer, 3:4, :])
        if reverse:
            return c_add(line(peer, 6), c_add(c_mul(line(peer, 12), left), c_mul(line(peer, 8), right)))
        return c_add(line(peer, 4), c_add(c_mul(line(peer, 8), left), c_mul(line(peer, 10), right)))

    carries(later, keep(4), peers, hop, close)


def labels_of(section, own_ref, other_ref):
    mine = lax.axis_index("sect")
    return lambda rows, lanes: jnp.where(mine == section, own_ref[0, rows, lanes], other_ref[0, rows, lanes])


def take_in(section, pair, value_in, screen_in, weight_ref, back_ref, operand_ref):
    for half in range(2):
        lanes = lanes_of(pair, half)
        line = line_of(back_ref, 2 * pair + half)
        for top in range(0, BLOCK, CHUNK):
            rows = slice(top, top + CHUNK)
            value = add_reach(weight_ref, section, rows, (value_in[0, rows, lanes], value_in[1, rows, lanes]), line)
            put_operand(operand_ref, 128 * half + top, *c_mul((screen_in[0, rows, lanes], screen_in[1, rows, lanes]), value))


def second_kernel(pairs, value_in, back_ref, screen_in, own_ref, other_ref, zone_ref, factor_ref, weight_ref, row_ref,
                  out_ref, sums_ref, screen_ref, operand_ref, grid_ref, edge_ref, carry_ref, late_ref, small_ref, line_ref, inner_ref):
    labels = labels_of(1, own_ref, other_ref)
    steps(
        pairs,
        lambda pair: take_in(0, pair, value_in, screen_in, weight_ref, back_ref, operand_ref.at[pair % SLOTS]),
        lambda pair: row_finish(0, operand_ref.at[pair % SLOTS], factor_ref, grid_ref, edge_ref, pair),
    )
    line_solve(0, back_ref, small_ref, line_ref, late_ref, factor_ref, row_ref, 2 * pairs)
    scan_rows(edge_ref, carry_ref, row_ref, 0, pairs)

    def turn(pair):
        out = multiply(factor_ref, 0, operand_ref.at[pair % SLOTS])
        for half in range(2):
            inner = slice(128 * half, 128 * half + 128)
            lanes = lanes_of(pair, half)
            line = line_of(late_ref, 2 * pair + half)
            for top in range(0, BLOCK, CHUNK):
                rows = slice(top, top + CHUNK)
                value = (out[rows, inner], out[top + BLOCK : top + BLOCK + CHUNK, inner])
                value = add_reach(weight_ref, 0, rows, value, line)
                screen = screen_at(row_ref, 1, labels(rows, lanes))
                screen_ref[0, rows, lanes] = screen[0]
                screen_ref[1, rows, lanes] = screen[1]
                zones = zone_ref[rows, lanes]
                value = c_mul((pick(row_ref, 1, 2, zones), pick(row_ref, 1, 3, zones)), c_mul(screen, value))
                put_operand(inner_ref.at[pair % SLOTS], 128 * half + top, *value)

    steps(
        pairs,
        lambda pair: column_stage(0, operand_ref.at[pair % SLOTS], weight_ref, carry_ref, grid_ref, pair),
        turn,
        lambda pair: row_finish(1, inner_ref.at[pair % SLOTS], factor_ref, grid_ref, edge_ref, pair),
    )
    scan_rows(edge_ref, carry_ref, row_ref, 1, pairs)

    def leave(pair):
        value = multiply(factor_ref, 1, operand_ref.at[pair % SLOTS])
        out_ref[0, :, wide_of(pair)] = value[0:128]
        out_ref[1, :, wide_of(pair)] = value[128:256]
        pack_edges(pair, value[256:264], sums_ref)

    steps(
        pairs,
        lambda pair: column_stage(1, operand_ref.at[pair % SLOTS], weight_ref, carry_ref, grid_ref, pair),
        leave,
        lambda pair: pack_sums(1, out_ref, screen_ref, pair, row_ref, weight_ref, sums_ref),
    )


def third_kernel(pairs, value_in, back_ref, screen_in, factor_ref, weight_ref, row_ref, out_ref,
                 operand_ref, grid_ref, edge_ref, carry_ref, late_ref, small_ref, line_ref):
    steps(
        pairs,
        lambda pair: take_in(1, pair, value_in, screen_in, weight_ref, back_ref, operand_ref.at[pair % SLOTS]),
        lambda pair: row_finish(1, operand_ref.at[pair % SLOTS], factor_ref, grid_ref, edge_ref, pair),
    )
    line_solve(1, back_ref, small_ref, line_ref, late_ref, factor_ref, row_ref, 2 * pairs)
    scan_rows(edge_ref, carry_ref, row_ref, 1, pairs)

    def leave(pair):
        out = multiply(factor_ref, 1, operand_ref.at[pair % SLOTS])
        for half in range(2):
            inner = slice(128 * half, 128 * half + 128)
            lanes = lanes_of(pair, half)
            line = line_of(late_ref, 2 * pair + half)
            for top in range(0, BLOCK, CHUNK):
                rows = slice(top, top + CHUNK)
                value = (out[rows, inner], out[top + BLOCK : top + BLOCK + CHUNK, inner])
                value = add_reach(weight_ref, 1, rows, value, line)
                out_ref[0, 0, rows, lanes] = value[0]
                out_ref[0, 1, rows, lanes] = value[1]

    steps(pairs, lambda pair: column_stage(1, operand_ref.at[pair % SLOTS], weight_ref, carry_ref, grid_ref, pair), leave)


ANY = pl.BlockSpec(memory_space=pl.ANY)
VMEM = pl.BlockSpec(memory_space=pltpu.VMEM)
SMEM = pl.BlockSpec(memory_space=pltpu.SMEM)


def call(body, in_specs, out_shape, scratch=()):
    out_specs = jax.tree.map(lambda _: VMEM, out_shape)
    return pl.pallas_call(
        body,
        in_specs=in_specs,
        out_specs=out_specs,
        out_shape=out_shape,
        scratch_shapes=list(scratch),
        compiler_params=pltpu.CompilerParams(vmem_limit_bytes=VMEM_LIMIT),
        interpret=INTERPRET,
    )


def shape(*sizes, kind=F32):
    return jax.ShapeDtypeStruct(sizes, kind)


def kernels(peers, width):
    pairs = width // 256
    passing = [
        pltpu.VMEM((SLOTS, 256, 512), BF16),
        pltpu.VMEM((pairs, 256, 256), F32),
        pltpu.VMEM((pairs, 8, 256), F32),
        pltpu.VMEM((2 * pairs, 8, BLOCK), F32),
    ]
    small = [pltpu.VMEM((2 * pairs, 8, BLOCK), F32), pltpu.VMEM((16 * pairs, 256), F32), pltpu.VMEM((16 * pairs, 384), F32)]
    grid = shape(2, BLOCK, width)
    grids = (grid, shape(peers, 16, BLOCK), grid)
    prepare = call(
        partial(prepare_kernel, width),
        [SMEM, SMEM, VMEM, VMEM, ANY, ANY],
        (
            shape(2, 384, 768, kind=BF16), shape(2, 12, BLOCK, BLOCK), shape(2, 8 * 14, BLOCK),
            grid, shape(1, BLOCK, width, kind=jnp.int32),
        ),
        [pltpu.VMEM((8, BLOCK), F32), pltpu.SemaphoreType.DMA((2,))],
    )
    first = call(partial(first_kernel, pairs), [VMEM] * 6, grids, passing)
    middle = [call(partial(middle_kernel, peers, section), [VMEM, VMEM], shape(peers, 8, BLOCK)) for section in range(2)]
    second = call(partial(second_kernel, pairs), [VMEM] * 9, grids, passing + small + passing[:1])
    third = call(partial(third_kernel, pairs), [VMEM] * 6, shape(1, 2, BLOCK, width), passing + small)
    return prepare, first, middle, second, third


def stay(value):
    return value if INTERPRET else pltpu.with_memory_space_constraint(value, pltpu.HBM)


def fast_shards(fields, region_ids, index_offsets, step_lengths, wave_numbers, zone_ids, zone_phases):
    prepare, first, middle, second, third = kernels(lax.axis_size("slab"), fields.shape[-1])
    other = lax.ppermute(region_ids, "sect", [(0, 1), (1, 0)])
    small = [stay(table) for table in (wave_numbers, step_lengths, index_offsets, zone_phases)]
    factor, weights, row, field, own = prepare(*small, stay(fields), stay(region_ids))

    def exchange(sums, section):
        held = lax.all_to_all(sums, "slab", 0, 0, tiled=True)
        return lax.all_to_all(middle[section](held, row), "slab", 0, 0, tiled=True)

    value, sums, screen = first(field, own, other, factor, weights, row)
    back = exchange(sums, 0)
    value, sums, screen = second(value, back, screen, own, other, zone_ids, factor, weights, row)
    back = exchange(sums, 1)
    return third(value, back, screen, factor, weights, row)


def choose(fields, *others):
    rows, width = fields.shape[-2:]
    if rows == BLOCK and width == BLOCK * lax.axis_size("slab") and lax.axis_size("sect") == 2:
        return fast_shards(fields, *others)
    return shards(fields, *others)


def solution(mesh):
    return jax.shard_map(
        choose,
        mesh=mesh,
        in_specs=(
            P(None, None, "slab", None),
            P("sect", "slab", None),
            P(),
            P(),
            P(),
            P("slab", None),
            P(),
        ),
        out_specs=P("sect", None, "slab", None),
        check_vma=False,
    )
```

```python
from functools import partial

import jax
import jax.numpy as jnp
from jax import lax
from jax.experimental import pallas as pl
from jax.experimental.pallas import tpu as pltpu
from jax.sharding import PartitionSpec as P

STEPS = 2
BLOCK = 128
INTERPRET = False
HIGHEST = lax.Precision.HIGHEST


def c_mul(a, b):
    return a[0] * b[0] - a[1] * b[1], a[0] * b[1] + a[1] * b[0]


def c_add(a, b):
    return a[0] + b[0], a[1] + b[1]


def c_div(a, b):
    size = b[0] * b[0] + b[1] * b[1]
    return (a[0] * b[0] + a[1] * b[1]) / size, (a[1] * b[0] - a[0] * b[1]) / size


def c_sqrt(a):
    size = jnp.sqrt(a[0] * a[0] + a[1] * a[1])
    real = jnp.sqrt(0.5 * (size + a[0]))
    return real, 0.5 * a[1] / real


def c_power(theta, count):
    size = jnp.exp(-theta[0] * count)
    angle = theta[1] * count
    return size * jnp.cos(angle), -size * jnp.sin(angle)


def scalars(number, length):
    sigma = number * length * 0.25
    size = 0.0625 + sigma * sigma
    square = number * number / size
    z = (-0.0625 * square, -0.25 * sigma * square)
    sinh = c_sqrt(z)
    cosh = c_sqrt((1.0 + z[0], z[1]))
    small = c_add(sinh, c_div(z, (1.0 + cosh[0], cosh[1])))
    theta = (
        jnp.log1p(2.0 * small[0] + small[0] * small[0] + small[1] * small[1]),
        2.0 * jnp.arctan2(small[1], 1.0 + small[0]),
    )
    front = (-2.0 * sigma * sigma / size, -0.5 * sigma / size)
    gamma = c_mul(front, c_div(sinh, cosh))
    alpha = ((0.0625 - sigma * sigma) / size, 0.5 * sigma / size)
    return theta, gamma, c_mul(alpha, alpha)


def closure(theta, total):
    power = c_power(theta, float(total))
    return c_div((jnp.ones_like(power[0]), jnp.zeros_like(power[0])), (1.0 - power[0], -power[1]))


def toeplitz(theta, gamma, count):
    index = jnp.arange(count, dtype=jnp.int32)
    apart = jnp.abs(index[:, None] - index[None, :])
    real, imaginary = c_mul(gamma, c_power(theta, apart.astype(jnp.float32)))
    return jnp.where(apart == 0, 1.0, 0.0) + real, imaginary


def circulant(theta, size, blocks):
    index = jnp.arange(blocks, dtype=jnp.int32)
    apart = jnp.mod(index[:, None] - index[None, :] - 1, blocks).astype(jnp.float32)
    return c_mul(closure(theta, size * blocks), c_power(theta, apart * size))


def c_ein(spec, a, b):
    def one(x, y):
        return jnp.einsum(spec, x, y, precision=HIGHEST)

    return one(a[0], b[0]) - one(a[1], b[1]), one(a[0], b[1]) + one(a[1], b[0])


def spans(theta, gamma, count):
    index = jnp.arange(count, dtype=jnp.int32).astype(jnp.float32)
    weight_left = c_mul(gamma, c_power(theta, count - 1 - index))
    weight_right = c_mul(gamma, c_power(theta, index))
    reach_left = c_power(theta, index + 1)
    reach_right = c_power(theta, count - index)
    return weight_left, weight_right, reach_left, reach_right


def row_solve(x, theta, gamma):
    shape = x[0].shape
    blocks = shape[-1] // BLOCK
    x = tuple(part.reshape(shape[:-1] + (blocks, BLOCK)) for part in x)
    weight_left, weight_right, reach_left, reach_right = spans(theta, gamma, BLOCK)
    ring = circulant(theta, BLOCK, blocks)
    y = c_ein("...bi,ij->...bj", x, toeplitz(theta, gamma, BLOCK))
    left = c_ein("...b,cb->...c", c_ein("...bi,i->...b", x, weight_left), ring)
    right = c_ein("...b,bc->...c", c_ein("...bi,i->...b", x, weight_right), ring)
    y = c_add(y, c_ein("...b,i->...bi", left, reach_left))
    y = c_add(y, c_ein("...b,i->...bi", right, reach_right))
    return tuple(part.reshape(shape) for part in y)


def pick_values(labels, table):
    picked = jnp.zeros(labels.shape, jnp.float32)
    for entry in range(table.shape[-1]):
        picked = picked + jnp.where(labels == entry, table[entry], 0.0)
    return picked


def column_local(x, theta, gamma, rows):
    weight_left, weight_right, _, _ = spans(theta, gamma, rows)
    y = c_ein("ij,jm->im", toeplitz(theta, gamma, rows), x)
    return y, c_ein("i,im->m", weight_left, x), c_ein("i,im->m", weight_right, x)


def reach(y, left, right, theta, gamma, rows):
    _, _, reach_left, reach_right = spans(theta, gamma, rows)
    y = c_add(y, c_ein("i,m->im", reach_left, left))
    return c_add(y, c_ein("i,m->im", reach_right, right))


def payload(y, left, right, screen, theta, gamma, rows):
    weight_left, weight_right, reach_left, reach_right = spans(theta, gamma, rows)
    z = c_mul(screen, y)
    parts = [left, right, c_ein("i,im->m", weight_left, z), c_ein("i,im->m", weight_right, z)]
    for weight, other in ((weight_left, reach_left), (weight_left, reach_right), (weight_right, reach_left)):
        parts.append(c_ein("i,im->m", c_mul(weight, other), screen))
    return jnp.stack([half for part in parts for half in part])


def exchange(packed, theta, rows):
    peers = lax.axis_size("slab")
    width = packed.shape[-1] // peers
    sent = jnp.swapaxes(packed.reshape(packed.shape[0], peers, width), 0, 1)
    held = lax.all_to_all(sent, "slab", 0, 0, tiled=True)
    one = [(held[:, 2 * i], held[:, 2 * i + 1]) for i in range(7)]
    ring = circulant(theta, rows, peers)
    left = c_ein("cb,bm->cm", ring, one[0])
    right = c_ein("bc,bm->cm", ring, one[1])
    next_left = c_add(one[2], c_add(c_mul(one[4], left), c_mul(one[5], right)))
    next_right = c_add(one[3], c_add(c_mul(one[6], left), c_mul(one[4], right)))
    next_left = c_ein("cb,bm->cm", ring, next_left)
    next_right = c_ein("bc,bm->cm", ring, next_right)
    back = jnp.stack([half for part in (left, right, next_left, next_right) for half in part], axis=1)
    back = lax.all_to_all(back, "slab", 0, 0, tiled=True)
    back = jnp.swapaxes(back, 0, 1).reshape(8, peers * width)
    return [(back[2 * i], back[2 * i + 1]) for i in range(4)]


def shards(fields, region_ids, index_offsets, step_lengths, wave_numbers, zone_ids, zone_phases):
    mine = lax.axis_index("sect")
    other = lax.ppermute(region_ids, "sect", [(0, 1), (1, 0)])
    labels = [jnp.where(mine == s, region_ids[0], other[0]) for s in range(2)]
    field = lax.dynamic_index_in_dim(fields, mine, 0, False)
    number = lax.dynamic_index_in_dim(wave_numbers, mine, 0, False)
    phases = lax.dynamic_index_in_dim(zone_phases, mine, 0, False)
    rows = field.shape[1]
    u = (field[0], field[1])
    lens = (pick_values(zone_ids, jnp.cos(phases)), pick_values(zone_ids, jnp.sin(phases)))
    for section in range(2):
        theta, gamma, turn = scalars(number, step_lengths[section])
        phase = number * step_lengths[section] * index_offsets[section]
        table = c_mul(turn, (jnp.cos(phase), jnp.sin(phase)))
        screen = tuple(pick_values(labels[section], half) for half in table)
        u = c_mul(u, screen)
        if section == 1:
            u = c_mul(u, lens)
        u, left, right = column_local(row_solve(u, theta, gamma), theta, gamma, rows)
        sent = payload(u, left, right, screen, theta, gamma, rows)
        back = exchange(sent, theta, rows)
        u = reach(u, back[0], back[1], theta, gamma, rows)
        u, _, _ = column_local(row_solve(c_mul(u, screen), theta, gamma), theta, gamma, rows)
        left = row_solve(back[2], theta, gamma)
        right = row_solve(back[3], theta, gamma)
        u = reach(u, left, right, theta, gamma, rows)
    return jnp.stack(u)[None]


F32 = jnp.float32
BF16 = jnp.bfloat16
LHS_ROWS = 272
SLOTS = 2

CHUNK = 32
VMEM_LIMIT = 22 * 1024 * 1024


def tile_of(value):
    return jnp.full((8, BLOCK), value, F32)


def grid_power(base, exponent, bits):
    real = jnp.ones(exponent.shape, F32)
    imaginary = jnp.zeros(exponent.shape, F32)
    for bit in range(bits):
        on = (exponent // (1 << bit)) % 2 == 1
        step = c_mul((real, imaginary), base)
        real = jnp.where(on, step[0], real)
        imaginary = jnp.where(on, step[1], imaginary)
        base = c_mul(base, base)
    return real, imaginary


def spread_to(pair, shape):
    return tuple(jnp.broadcast_to(part[0:1, 0:1], shape) for part in pair)


def prepare_kernel(total, number_ref, length_ref, offset_ref, zone_ref, field_any, label_any,
                   factor_ref, weight_ref, row_ref, field_ref, label_ref, pad_ref, sems):
    mine = lax.axis_index("sect")
    copies = [
        pltpu.make_async_copy(field_any.at[mine], field_ref, sems.at[0]),
        pltpu.make_async_copy(label_any, label_ref, sems.at[1]),
    ]
    for copy in copies:
        copy.start()
    number = tile_of(number_ref[mine])
    tall = (BLOCK, BLOCK)
    place = lax.broadcasted_iota(jnp.int32, tall, 0)
    across = lax.broadcasted_iota(jnp.int32, tall, 1)
    lane = lax.broadcasted_iota(jnp.int32, (8, BLOCK), 1)
    pad_ref[...] = jnp.zeros((8, BLOCK), F32)
    pad_ref[0:2, 0 : offset_ref.shape[1]] = offset_ref[...]
    pad_ref[2:3, 0 : zone_ref.shape[1]] = zone_ref[pl.ds(mine, 1), :]
    lens = jnp.broadcast_to(pad_ref[2:3, :], (8, BLOCK))
    lens = (jnp.cos(lens), jnp.sin(lens))

    def keep(section, top, bottom, real, imaginary):
        for first, value in ((0, real), (BLOCK, imaginary)):
            high, low = split(value)
            factor_ref[section, top:bottom, first : first + BLOCK] = high
            factor_ref[section, top:bottom, 256 + first : 256 + first + BLOCK] = low
            factor_ref[section, top:bottom, 512 + first : 512 + first + BLOCK] = high

    for section in range(2):
        length = tile_of(length_ref[section])
        sigma = number * length * 0.25
        size = 0.0625 + sigma * sigma
        square = number * number / size
        z = (-0.0625 * square, -0.25 * sigma * square)
        sinh = c_sqrt(z)
        cosh = c_sqrt((1.0 + z[0], z[1]))
        root = (cosh[0] - sinh[0], cosh[1] - sinh[1])
        base = c_mul(root, root)
        gamma = c_mul((-2.0 * sigma * sigma / size, -0.5 * sigma / size), c_div(sinh, cosh))
        alpha = ((0.0625 - sigma * sigma) / size, 0.5 * sigma / size)
        turn = c_mul(alpha, alpha)
        hop = base
        for _ in range(7):
            hop = c_mul(hop, hop)
        whole = hop
        for _ in range(total.bit_length() - 8):
            whole = c_mul(whole, whole)
        close = c_div((jnp.ones_like(whole[0]), jnp.zeros_like(whole[0])), (1.0 - whole[0], -whole[1]))
        wide = spread_to(base, tall)
        gain = spread_to(gamma, tall)
        real, imaginary = c_mul(gain, grid_power(wide, jnp.abs(place - across), 7))
        real = real + jnp.where(place == across, 1.0, 0.0)
        keep(section, 0, 128, real, -imaginary)
        keep(section, 128, 256, imaginary, real)
        ahead = grid_power(base, lane, 7)
        behind = grid_power(base, 127 - lane, 7)
        left = c_mul(gamma, behind)
        right = c_mul(gamma, ahead)
        row = lax.broadcasted_iota(jnp.int32, (16, BLOCK), 0)

        def four(values):
            out = jnp.zeros((16, BLOCK), F32)
            for index, value in enumerate(values):
                out = jnp.where(row == index, jnp.broadcast_to(value[0:1], (16, BLOCK)), out)
            return out

        keep(section, 256, 272, four((left[0], left[1], right[0], right[1])), four((-left[1], left[0], -right[1], right[0])))
        factor_ref[section, 272:384, :] = jnp.zeros((112, 768), BF16)
        phase = number * length * jnp.broadcast_to(pad_ref[section : section + 1, :], (8, BLOCK))
        screen = c_mul(turn, (jnp.cos(phase), jnp.sin(phase)))
        reach_left = c_mul(base, ahead)
        reach_right = c_mul(base, behind)
        both = c_mul(gamma, hop)
        listed = [*screen, *lens, *reach_left, *reach_right, *hop, *close, *both]
        for index, value in enumerate(listed):
            row_ref[section, 8 * index : 8 * index + 8, :] = value
        down = grid_power(wide, place, 7)
        up = grid_power(wide, 127 - place, 7)
        high = c_mul(wide, down)
        low = c_mul(wide, up)
        from_left = c_mul(gain, up)
        from_right = c_mul(gain, down)
        tables = [high, low, from_left, from_right, c_mul(from_left, low), c_mul(from_right, high)]
        for index, table in enumerate(tables):
            weight_ref[section, 2 * index] = table[0]
            weight_ref[section, 2 * index + 1] = table[1]
    for copy in copies:
        copy.wait()


def split(value):
    high = value.astype(BF16)
    return high, (value - high.astype(F32)).astype(BF16)


def put_operand(operand_ref, top, real, imaginary):
    size = real.shape[0]
    high, low = split(real)
    operand_ref[top : top + size, 0:128] = high
    operand_ref[top : top + size, 256:384] = low
    high, low = split(imaginary)
    operand_ref[top : top + size, 128:256] = high
    operand_ref[top : top + size, 384:512] = low


def multiply(factor_ref, section, operand_ref):
    high = operand_ref[:, 0:256]
    right = jnp.concatenate([high, high, operand_ref[:, 256:512]], axis=1)
    return lax.dot_general(factor_ref[section, 0:LHS_ROWS, :], right, (((1,), (1,)), ((), ())), preferred_element_type=F32)


def reach_of(weight_ref, section, rows):
    return [weight_ref[section, index, rows, :] for index in range(4)]


def add_reach(table, value, line):
    high, low = table[0:2], table[2:4]
    return c_add(value, c_add(c_mul(high, (line[0], line[1])), c_mul(low, (line[2], line[3]))))


def line_of(carry_ref, block):
    return [carry_ref[block, part : part + 1, :] for part in range(4)]


def pick(table_ref, section, index, labels):
    table = jnp.broadcast_to(table_ref[section, 8 * index : 8 * index + 1, :], labels.shape)
    return jnp.take_along_axis(table, labels, axis=1, mode="promise_in_bounds")


def screen_at(row_ref, section, labels):
    return pick(row_ref, section, 0, labels), pick(row_ref, section, 1, labels)


def row_line(row_ref, section, index):
    return row_ref[section, 8 * index : 8 * index + 1, :]


def hop_of(row_ref, section):
    return (row_line(row_ref, section, 8), row_line(row_ref, section, 9)), (row_line(row_ref, section, 10), row_line(row_ref, section, 11))


def carries(get, put, count, hop, close):
    for reverse in (False, True):
        order = list(range(count))[:: -1 if reverse else 1]
        total = get(order[0], reverse)
        for index in order[1:]:
            total = c_add(c_mul(hop, total), get(index, reverse))
        carry = c_mul(close, total)
        for index in order:
            put(index, reverse, carry)
            carry = c_add(c_mul(hop, carry), get(index, reverse))


def scan_rows(edge_ref, carry_ref, row_ref, section, pairs):
    hop, close = hop_of(row_ref, section)

    def get(block, reverse):
        first = 2 if reverse else 0
        lanes = slice(128 * (block % 2), 128 * (block % 2) + 128)
        return tuple(edge_ref[block // 2, first + part : first + part + 1, lanes] for part in range(2))

    def put(block, reverse, value):
        for part in range(2):
            first = (2 if reverse else 0) + part
            carry_ref[block, first : first + 1, :] = value[part]

    carries(get, put, 2 * pairs, hop, close)


def row_finish(section, operand_ref, factor_ref, grid_ref, edge_ref, pair):
    out = multiply(factor_ref, section, operand_ref)
    grid_ref[pair] = out[0:256]
    edge_ref[pair] = out[256:264]


def column_stage(section, operand_ref, weight_ref, carry_ref, grid_ref, pair):
    lines = [line_of(carry_ref, 2 * pair + half) for half in range(2)]
    for top in range(0, BLOCK, CHUNK):
        rows = slice(top, top + CHUNK)
        table = reach_of(weight_ref, section, rows)
        for half in range(2):
            lanes = slice(128 * half, 128 * half + 128)
            value = (grid_ref[pair, rows, lanes], grid_ref[pair, top + BLOCK : top + BLOCK + CHUNK, lanes])
            put_operand(operand_ref, 128 * half + top, *add_reach(table, value, lines[half]))


def pack_edges(pair, ends, sums_ref):
    for half in range(2):
        sums_ref[2 * pair + half, 0:4, :] = ends[0:4, 128 * half : 128 * half + 128]


def pack_sums(section, out_ref, screen_ref, pair, row_ref, weight_ref, sums_ref):
    for half in range(2):
        block = 2 * pair + half
        lanes = lanes_of(pair, half)
        sums = [jnp.zeros((8, BLOCK), F32) for _ in range(10)]
        for top in range(0, BLOCK, 8):
            rows = slice(top, top + 8)
            screen = (screen_ref[0, rows, lanes], screen_ref[1, rows, lanes])
            value = c_mul(screen, (out_ref[0, rows, lanes], out_ref[1, rows, lanes]))
            weights = [(weight_ref[section, 2 * k, rows, :], weight_ref[section, 2 * k + 1, rows, :]) for k in range(2, 6)]
            terms = (c_mul(weights[0], value), c_mul(weights[1], value), screen, c_mul(weights[2], screen), c_mul(weights[3], screen))
            for k, term in enumerate(terms):
                sums[2 * k] = sums[2 * k] + term[0]
                sums[2 * k + 1] = sums[2 * k + 1] + term[1]
        lines = [jnp.sum(part, axis=0, keepdims=True) for part in sums]
        both = c_mul((row_line(row_ref, section, 12), row_line(row_ref, section, 13)), (lines[4], lines[5]))
        for k, line in enumerate(lines[0:4] + list(both) + lines[6:10]):
            sums_ref[block, 4 + k : 5 + k, :] = line
        sums_ref[block, 14:16, :] = jnp.zeros((2, BLOCK), F32)


def line_solve(section, back_ref, small_ref, line_ref, carry_ref, factor_ref, row_ref, blocks):
    small_ref[...] = jnp.zeros(small_ref.shape, F32)
    for block in range(blocks):
        for side in range(2):
            for part in range(2):
                row = 4 + 2 * side + part
                small_ref[8 * block + side : 8 * block + side + 1, 128 * part : 128 * part + 128] = back_ref[block, row : row + 1, :]
    high, low = split(small_ref[...])
    left = jnp.concatenate([high, high, low], axis=1)
    out = lax.dot_general(left, factor_ref[section], (((1,), (1,)), ((), ())), preferred_element_type=F32)
    line_ref[...] = out
    wide = (8, BLOCK)
    hop, close = (tuple(jnp.broadcast_to(part, wide) for part in pair) for pair in hop_of(row_ref, section))
    reach_left = tuple(row_ref[section, 8 * k : 8 * k + 8, :] for k in (4, 5))
    reach_right = tuple(row_ref[section, 8 * k : 8 * k + 8, :] for k in (6, 7))

    def get(block, reverse):
        first = 258 if reverse else 256
        rows = slice(8 * block, 8 * block + 8)
        return tuple(jnp.broadcast_to(line_ref[rows, first + part : first + part + 1], wide) for part in range(2))

    def put(block, reverse, value):
        rows = slice(8 * block, 8 * block + 8)
        add = c_mul(reach_right if reverse else reach_left, value)
        real = line_ref[rows, 0:128] + add[0]
        imaginary = line_ref[rows, 128:256] + add[1]
        if not reverse:
            line_ref[rows, 0:128] = real
            line_ref[rows, 128:256] = imaginary
        else:
            for side in range(2):
                carry_ref[block, 2 * side : 2 * side + 1, :] = real[side : side + 1]
                carry_ref[block, 2 * side + 1 : 2 * side + 2, :] = imaginary[side : side + 1]

    carries(get, put, blocks, hop, close)


def lanes_of(pair, half):
    return slice(256 * pair + 128 * half, 256 * pair + 128 * half + 128)


def wide_of(pair):
    return slice(256 * pair, 256 * pair + 256)


def steps(count, *bodies):
    for time in range(count + len(bodies) - 1):
        for depth, body in enumerate(bodies):
            if 0 <= time - depth < count:
                body(time - depth)


def first_kernel(pairs, field_ref, own_ref, other_ref, factor_ref, weight_ref, row_ref, out_ref, sums_ref, screen_ref,
                 operand_ref, grid_ref, edge_ref, carry_ref):
    labels = labels_of(0, own_ref, other_ref)

    def stage(pair):
        for half in range(2):
            lanes = lanes_of(pair, half)
            for top in range(0, BLOCK, CHUNK):
                rows = slice(top, top + CHUNK)
                screen = screen_at(row_ref, 0, labels(rows, lanes))
                screen_ref[0, rows, lanes] = screen[0]
                screen_ref[1, rows, lanes] = screen[1]
                value = c_mul(screen, (field_ref[0, rows, lanes], field_ref[1, rows, lanes]))
                put_operand(operand_ref.at[pair % SLOTS], 128 * half + top, *value)

    steps(pairs, stage, lambda pair: row_finish(0, operand_ref.at[pair % SLOTS], factor_ref, grid_ref, edge_ref, pair))
    scan_rows(edge_ref, carry_ref, row_ref, 0, pairs)

    def leave(pair):
        value = multiply(factor_ref, 0, operand_ref.at[pair % SLOTS])
        out_ref[0, :, wide_of(pair)] = value[0:128]
        out_ref[1, :, wide_of(pair)] = value[128:256]
        pack_edges(pair, value[256:264], sums_ref)

    steps(
        pairs,
        lambda pair: column_stage(0, operand_ref.at[pair % SLOTS], weight_ref, carry_ref, grid_ref, pair),
        leave,
        lambda pair: pack_sums(0, out_ref, screen_ref, pair, row_ref, weight_ref, sums_ref),
    )


def middle_kernel(peers, section, held_ref, row_ref, back_ref):
    hop, close = hop_of(row_ref, section)

    def line(peer, row):
        return held_ref[peer, row : row + 1, :], held_ref[peer, row + 1 : row + 2, :]

    def keep(first):
        def put(peer, reverse, value):
            row = first + (2 if reverse else 0)
            back_ref[peer, row : row + 1, :] = value[0]
            back_ref[peer, row + 1 : row + 2, :] = value[1]

        return put

    carries(lambda peer, reverse: line(peer, 2 if reverse else 0), keep(0), peers, hop, close)

    def later(peer, reverse):
        left = (back_ref[peer, 0:1, :], back_ref[peer, 1:2, :])
        right = (back_ref[peer, 2:3, :], back_ref[peer, 3:4, :])
        if reverse:
            return c_add(line(peer, 6), c_add(c_mul(line(peer, 12), left), c_mul(line(peer, 8), right)))
        return c_add(line(peer, 4), c_add(c_mul(line(peer, 8), left), c_mul(line(peer, 10), right)))

    carries(later, keep(4), peers, hop, close)


def labels_of(section, own_ref, other_ref):
    mine = lax.axis_index("sect")
    return lambda rows, lanes: jnp.where(mine == section, own_ref[0, rows, lanes], other_ref[0, rows, lanes])


def take_in(section, pair, value_in, screen_in, weight_ref, back_ref, operand_ref):
    lines = [line_of(back_ref, 2 * pair + half) for half in range(2)]
    for top in range(0, BLOCK, CHUNK):
        rows = slice(top, top + CHUNK)
        table = reach_of(weight_ref, section, rows)
        for half in range(2):
            lanes = lanes_of(pair, half)
            value = add_reach(table, (value_in[0, rows, lanes], value_in[1, rows, lanes]), lines[half])
            put_operand(operand_ref, 128 * half + top, *c_mul((screen_in[0, rows, lanes], screen_in[1, rows, lanes]), value))


def second_kernel(pairs, value_in, back_ref, screen_in, own_ref, other_ref, zone_ref, factor_ref, weight_ref, row_ref,
                  out_ref, sums_ref, screen_ref, operand_ref, grid_ref, edge_ref, carry_ref, late_ref, small_ref, line_ref, inner_ref):
    labels = labels_of(1, own_ref, other_ref)
    steps(
        pairs,
        lambda pair: take_in(0, pair, value_in, screen_in, weight_ref, back_ref, operand_ref.at[pair % SLOTS]),
        lambda pair: row_finish(0, operand_ref.at[pair % SLOTS], factor_ref, grid_ref, edge_ref, pair),
    )
    line_solve(0, back_ref, small_ref, line_ref, late_ref, factor_ref, row_ref, 2 * pairs)
    scan_rows(edge_ref, carry_ref, row_ref, 0, pairs)

    def turn(pair):
        out = multiply(factor_ref, 0, operand_ref.at[pair % SLOTS])
        lines = [line_of(late_ref, 2 * pair + half) for half in range(2)]
        for top in range(0, BLOCK, CHUNK):
            rows = slice(top, top + CHUNK)
            table = reach_of(weight_ref, 0, rows)
            for half in range(2):
                inner = slice(128 * half, 128 * half + 128)
                lanes = lanes_of(pair, half)
                value = (out[rows, inner], out[top + BLOCK : top + BLOCK + CHUNK, inner])
                value = add_reach(table, value, lines[half])
                screen = screen_at(row_ref, 1, labels(rows, lanes))
                screen_ref[0, rows, lanes] = screen[0]
                screen_ref[1, rows, lanes] = screen[1]
                zones = zone_ref[rows, lanes]
                value = c_mul((pick(row_ref, 1, 2, zones), pick(row_ref, 1, 3, zones)), c_mul(screen, value))
                put_operand(inner_ref.at[pair % SLOTS], 128 * half + top, *value)

    steps(
        pairs,
        lambda pair: column_stage(0, operand_ref.at[pair % SLOTS], weight_ref, carry_ref, grid_ref, pair),
        turn,
        lambda pair: row_finish(1, inner_ref.at[pair % SLOTS], factor_ref, grid_ref, edge_ref, pair),
    )
    scan_rows(edge_ref, carry_ref, row_ref, 1, pairs)

    def leave(pair):
        value = multiply(factor_ref, 1, operand_ref.at[pair % SLOTS])
        out_ref[0, :, wide_of(pair)] = value[0:128]
        out_ref[1, :, wide_of(pair)] = value[128:256]
        pack_edges(pair, value[256:264], sums_ref)

    steps(
        pairs,
        lambda pair: column_stage(1, operand_ref.at[pair % SLOTS], weight_ref, carry_ref, grid_ref, pair),
        leave,
        lambda pair: pack_sums(1, out_ref, screen_ref, pair, row_ref, weight_ref, sums_ref),
    )


def third_kernel(pairs, value_in, back_ref, screen_in, factor_ref, weight_ref, row_ref, out_any,
                 operand_ref, grid_ref, edge_ref, carry_ref, late_ref, small_ref, line_ref, out_ref, sems):
    def write(pair):
        wide = wide_of(pair)
        return pltpu.make_async_copy(out_ref.at[:, :, wide], out_any.at[0, :, :, wide], sems.at[pair])

    steps(
        pairs,
        lambda pair: take_in(1, pair, value_in, screen_in, weight_ref, back_ref, operand_ref.at[pair % SLOTS]),
        lambda pair: row_finish(1, operand_ref.at[pair % SLOTS], factor_ref, grid_ref, edge_ref, pair),
    )
    line_solve(1, back_ref, small_ref, line_ref, late_ref, factor_ref, row_ref, 2 * pairs)
    scan_rows(edge_ref, carry_ref, row_ref, 1, pairs)

    def leave(pair):
        out = multiply(factor_ref, 1, operand_ref.at[pair % SLOTS])
        lines = [line_of(late_ref, 2 * pair + half) for half in range(2)]
        for top in range(0, BLOCK, CHUNK):
            rows = slice(top, top + CHUNK)
            table = reach_of(weight_ref, 1, rows)
            for half in range(2):
                inner = slice(128 * half, 128 * half + 128)
                lanes = lanes_of(pair, half)
                value = (out[rows, inner], out[top + BLOCK : top + BLOCK + CHUNK, inner])
                value = add_reach(table, value, lines[half])
                out_ref[0, rows, lanes] = value[0]
                out_ref[1, rows, lanes] = value[1]
        write(pair).start()

    steps(pairs, lambda pair: column_stage(1, operand_ref.at[pair % SLOTS], weight_ref, carry_ref, grid_ref, pair), leave)
    for pair in range(pairs):
        write(pair).wait()


ANY = pl.BlockSpec(memory_space=pl.ANY)
VMEM = pl.BlockSpec(memory_space=pltpu.VMEM)
SMEM = pl.BlockSpec(memory_space=pltpu.SMEM)


def call(body, in_specs, out_shape, scratch=(), out_space=VMEM):
    out_specs = jax.tree.map(lambda _: out_space, out_shape)
    return pl.pallas_call(
        body,
        in_specs=in_specs,
        out_specs=out_specs,
        out_shape=out_shape,
        scratch_shapes=list(scratch),
        compiler_params=pltpu.CompilerParams(vmem_limit_bytes=VMEM_LIMIT),
        interpret=INTERPRET,
    )


def shape(*sizes, kind=F32):
    return jax.ShapeDtypeStruct(sizes, kind)


def kernels(peers, width):
    pairs = width // 256
    passing = [
        pltpu.VMEM((SLOTS, 256, 512), BF16),
        pltpu.VMEM((pairs, 256, 256), F32),
        pltpu.VMEM((pairs, 8, 256), F32),
        pltpu.VMEM((2 * pairs, 8, BLOCK), F32),
    ]
    small = [pltpu.VMEM((2 * pairs, 8, BLOCK), F32), pltpu.VMEM((16 * pairs, 256), F32), pltpu.VMEM((16 * pairs, 384), F32)]
    grid = shape(2, BLOCK, width)
    grids = (grid, shape(peers, 16, BLOCK), grid)
    prepare = call(
        partial(prepare_kernel, width),
        [SMEM, SMEM, VMEM, VMEM, ANY, ANY],
        (
            shape(2, 384, 768, kind=BF16), shape(2, 12, BLOCK, BLOCK), shape(2, 8 * 14, BLOCK),
            grid, shape(1, BLOCK, width, kind=jnp.int32),
        ),
        [pltpu.VMEM((8, BLOCK), F32), pltpu.SemaphoreType.DMA((2,))],
    )
    first = call(partial(first_kernel, pairs), [VMEM] * 6, grids, passing)
    middle = [call(partial(middle_kernel, peers, section), [VMEM, VMEM], shape(peers, 8, BLOCK)) for section in range(2)]
    second = call(partial(second_kernel, pairs), [VMEM] * 9, grids, passing + small + passing[:1])
    third = call(partial(third_kernel, pairs), [VMEM] * 6, shape(1, 2, BLOCK, width),
                 passing + small + [pltpu.VMEM((2, BLOCK, width), F32), pltpu.SemaphoreType.DMA((pairs,))], ANY)
    return prepare, first, middle, second, third


def stay(value):
    return value if INTERPRET else pltpu.with_memory_space_constraint(value, pltpu.HBM)


def fast_shards(fields, region_ids, index_offsets, step_lengths, wave_numbers, zone_ids, zone_phases):
    prepare, first, middle, second, third = kernels(lax.axis_size("slab"), fields.shape[-1])
    other = lax.ppermute(region_ids, "sect", [(0, 1), (1, 0)])
    small = [stay(table) for table in (wave_numbers, step_lengths, index_offsets, zone_phases)]
    factor, weights, row, field, own = prepare(*small, stay(fields), stay(region_ids))

    def exchange(sums, section):
        held = lax.all_to_all(sums, "slab", 0, 0, tiled=True)
        return lax.all_to_all(middle[section](held, row), "slab", 0, 0, tiled=True)

    value, sums, screen = first(field, own, other, factor, weights, row)
    back = exchange(sums, 0)
    value, sums, screen = second(value, back, screen, own, other, zone_ids, factor, weights, row)
    back = exchange(sums, 1)
    return third(value, back, screen, factor, weights, row)


def choose(fields, *others):
    rows, width = fields.shape[-2:]
    if rows == BLOCK and width == BLOCK * lax.axis_size("slab") and lax.axis_size("sect") == 2:
        return fast_shards(fields, *others)
    return shards(fields, *others)


def solution(mesh):
    return jax.shard_map(
        choose,
        mesh=mesh,
        in_specs=(
            P(None, None, "slab", None),
            P("sect", "slab", None),
            P(),
            P(),
            P(),
            P("slab", None),
            P(),
        ),
        out_specs=P("sect", None, "slab", None),
        check_vma=False,
    )
```

```python
from functools import partial

import jax
import jax.numpy as jnp
from jax import lax
from jax.experimental import pallas as pl
from jax.experimental.pallas import tpu as pltpu
from jax.sharding import PartitionSpec as P

STEPS = 2
BLOCK = 128
INTERPRET = False
HIGHEST = lax.Precision.HIGHEST


def c_mul(a, b):
    return a[0] * b[0] - a[1] * b[1], a[0] * b[1] + a[1] * b[0]


def c_add(a, b):
    return a[0] + b[0], a[1] + b[1]


def c_div(a, b):
    size = b[0] * b[0] + b[1] * b[1]
    return (a[0] * b[0] + a[1] * b[1]) / size, (a[1] * b[0] - a[0] * b[1]) / size


def c_sqrt(a):
    size = jnp.sqrt(a[0] * a[0] + a[1] * a[1])
    real = jnp.sqrt(0.5 * (size + a[0]))
    return real, 0.5 * a[1] / real


def c_power(theta, count):
    size = jnp.exp(-theta[0] * count)
    angle = theta[1] * count
    return size * jnp.cos(angle), -size * jnp.sin(angle)


def scalars(number, length):
    sigma = number * length * 0.25
    size = 0.0625 + sigma * sigma
    square = number * number / size
    z = (-0.0625 * square, -0.25 * sigma * square)
    sinh = c_sqrt(z)
    cosh = c_sqrt((1.0 + z[0], z[1]))
    small = c_add(sinh, c_div(z, (1.0 + cosh[0], cosh[1])))
    theta = (
        jnp.log1p(2.0 * small[0] + small[0] * small[0] + small[1] * small[1]),
        2.0 * jnp.arctan2(small[1], 1.0 + small[0]),
    )
    front = (-2.0 * sigma * sigma / size, -0.5 * sigma / size)
    gamma = c_mul(front, c_div(sinh, cosh))
    alpha = ((0.0625 - sigma * sigma) / size, 0.5 * sigma / size)
    return theta, gamma, c_mul(alpha, alpha)


def closure(theta, total):
    power = c_power(theta, float(total))
    return c_div((jnp.ones_like(power[0]), jnp.zeros_like(power[0])), (1.0 - power[0], -power[1]))


def toeplitz(theta, gamma, count):
    index = jnp.arange(count, dtype=jnp.int32)
    apart = jnp.abs(index[:, None] - index[None, :])
    real, imaginary = c_mul(gamma, c_power(theta, apart.astype(jnp.float32)))
    return jnp.where(apart == 0, 1.0, 0.0) + real, imaginary


def circulant(theta, size, blocks):
    index = jnp.arange(blocks, dtype=jnp.int32)
    apart = jnp.mod(index[:, None] - index[None, :] - 1, blocks).astype(jnp.float32)
    return c_mul(closure(theta, size * blocks), c_power(theta, apart * size))


def c_ein(spec, a, b):
    def one(x, y):
        return jnp.einsum(spec, x, y, precision=HIGHEST)

    return one(a[0], b[0]) - one(a[1], b[1]), one(a[0], b[1]) + one(a[1], b[0])


def spans(theta, gamma, count):
    index = jnp.arange(count, dtype=jnp.int32).astype(jnp.float32)
    weight_left = c_mul(gamma, c_power(theta, count - 1 - index))
    weight_right = c_mul(gamma, c_power(theta, index))
    reach_left = c_power(theta, index + 1)
    reach_right = c_power(theta, count - index)
    return weight_left, weight_right, reach_left, reach_right


def row_solve(x, theta, gamma):
    shape = x[0].shape
    blocks = shape[-1] // BLOCK
    x = tuple(part.reshape(shape[:-1] + (blocks, BLOCK)) for part in x)
    weight_left, weight_right, reach_left, reach_right = spans(theta, gamma, BLOCK)
    ring = circulant(theta, BLOCK, blocks)
    y = c_ein("...bi,ij->...bj", x, toeplitz(theta, gamma, BLOCK))
    left = c_ein("...b,cb->...c", c_ein("...bi,i->...b", x, weight_left), ring)
    right = c_ein("...b,bc->...c", c_ein("...bi,i->...b", x, weight_right), ring)
    y = c_add(y, c_ein("...b,i->...bi", left, reach_left))
    y = c_add(y, c_ein("...b,i->...bi", right, reach_right))
    return tuple(part.reshape(shape) for part in y)


def pick_values(labels, table):
    picked = jnp.zeros(labels.shape, jnp.float32)
    for entry in range(table.shape[-1]):
        picked = picked + jnp.where(labels == entry, table[entry], 0.0)
    return picked


def column_local(x, theta, gamma, rows):
    weight_left, weight_right, _, _ = spans(theta, gamma, rows)
    y = c_ein("ij,jm->im", toeplitz(theta, gamma, rows), x)
    return y, c_ein("i,im->m", weight_left, x), c_ein("i,im->m", weight_right, x)


def reach(y, left, right, theta, gamma, rows):
    _, _, reach_left, reach_right = spans(theta, gamma, rows)
    y = c_add(y, c_ein("i,m->im", reach_left, left))
    return c_add(y, c_ein("i,m->im", reach_right, right))


def payload(y, left, right, screen, theta, gamma, rows):
    weight_left, weight_right, reach_left, reach_right = spans(theta, gamma, rows)
    z = c_mul(screen, y)
    parts = [left, right, c_ein("i,im->m", weight_left, z), c_ein("i,im->m", weight_right, z)]
    for weight, other in ((weight_left, reach_left), (weight_left, reach_right), (weight_right, reach_left)):
        parts.append(c_ein("i,im->m", c_mul(weight, other), screen))
    return jnp.stack([half for part in parts for half in part])


def exchange(packed, theta, rows):
    peers = lax.axis_size("slab")
    width = packed.shape[-1] // peers
    sent = jnp.swapaxes(packed.reshape(packed.shape[0], peers, width), 0, 1)
    held = lax.all_to_all(sent, "slab", 0, 0, tiled=True)
    one = [(held[:, 2 * i], held[:, 2 * i + 1]) for i in range(7)]
    ring = circulant(theta, rows, peers)
    left = c_ein("cb,bm->cm", ring, one[0])
    right = c_ein("bc,bm->cm", ring, one[1])
    next_left = c_add(one[2], c_add(c_mul(one[4], left), c_mul(one[5], right)))
    next_right = c_add(one[3], c_add(c_mul(one[6], left), c_mul(one[4], right)))
    next_left = c_ein("cb,bm->cm", ring, next_left)
    next_right = c_ein("bc,bm->cm", ring, next_right)
    back = jnp.stack([half for part in (left, right, next_left, next_right) for half in part], axis=1)
    back = lax.all_to_all(back, "slab", 0, 0, tiled=True)
    back = jnp.swapaxes(back, 0, 1).reshape(8, peers * width)
    return [(back[2 * i], back[2 * i + 1]) for i in range(4)]


def shards(fields, region_ids, index_offsets, step_lengths, wave_numbers, zone_ids, zone_phases):
    mine = lax.axis_index("sect")
    other = lax.ppermute(region_ids, "sect", [(0, 1), (1, 0)])
    labels = [jnp.where(mine == s, region_ids[0], other[0]) for s in range(2)]
    field = lax.dynamic_index_in_dim(fields, mine, 0, False)
    number = lax.dynamic_index_in_dim(wave_numbers, mine, 0, False)
    phases = lax.dynamic_index_in_dim(zone_phases, mine, 0, False)
    rows = field.shape[1]
    u = (field[0], field[1])
    lens = (pick_values(zone_ids, jnp.cos(phases)), pick_values(zone_ids, jnp.sin(phases)))
    for section in range(2):
        theta, gamma, turn = scalars(number, step_lengths[section])
        phase = number * step_lengths[section] * index_offsets[section]
        table = c_mul(turn, (jnp.cos(phase), jnp.sin(phase)))
        screen = tuple(pick_values(labels[section], half) for half in table)
        u = c_mul(u, screen)
        if section == 1:
            u = c_mul(u, lens)
        u, left, right = column_local(row_solve(u, theta, gamma), theta, gamma, rows)
        sent = payload(u, left, right, screen, theta, gamma, rows)
        back = exchange(sent, theta, rows)
        u = reach(u, back[0], back[1], theta, gamma, rows)
        u, _, _ = column_local(row_solve(c_mul(u, screen), theta, gamma), theta, gamma, rows)
        left = row_solve(back[2], theta, gamma)
        right = row_solve(back[3], theta, gamma)
        u = reach(u, left, right, theta, gamma, rows)
    return jnp.stack(u)[None]


F32 = jnp.float32
BF16 = jnp.bfloat16
LHS_ROWS = 272
SLOTS = 2

CHUNK = 32
VMEM_LIMIT = 22 * 1024 * 1024


def tile_of(value):
    return jnp.full((8, BLOCK), value, F32)


def grid_power(base, exponent, bits):
    real = jnp.ones(exponent.shape, F32)
    imaginary = jnp.zeros(exponent.shape, F32)
    for bit in range(bits):
        on = (exponent // (1 << bit)) % 2 == 1
        step = c_mul((real, imaginary), base)
        real = jnp.where(on, step[0], real)
        imaginary = jnp.where(on, step[1], imaginary)
        base = c_mul(base, base)
    return real, imaginary


def spread_to(pair, shape):
    return tuple(jnp.broadcast_to(part[0:1, 0:1], shape) for part in pair)


def prepare_kernel(total, number_ref, length_ref, offset_ref, zone_ref, field_any, label_any,
                   factor_ref, weight_ref, row_ref, field_ref, label_ref, pad_ref, sems):
    mine = lax.axis_index("sect")
    copies = [
        pltpu.make_async_copy(field_any.at[mine], field_ref, sems.at[0]),
        pltpu.make_async_copy(label_any, label_ref, sems.at[1]),
    ]
    for copy in copies:
        copy.start()
    number = tile_of(number_ref[mine])
    tall = (BLOCK, BLOCK)
    place = lax.broadcasted_iota(jnp.int32, tall, 0)
    across = lax.broadcasted_iota(jnp.int32, tall, 1)
    lane = lax.broadcasted_iota(jnp.int32, (8, BLOCK), 1)
    pad_ref[...] = jnp.zeros((8, BLOCK), F32)
    pad_ref[0:2, 0 : offset_ref.shape[1]] = offset_ref[...]
    pad_ref[2:3, 0 : zone_ref.shape[1]] = zone_ref[pl.ds(mine, 1), :]
    lens = jnp.broadcast_to(pad_ref[2:3, :], (8, BLOCK))
    lens = (jnp.cos(lens), jnp.sin(lens))

    def keep(section, top, bottom, real, imaginary):
        for first, value in ((0, real), (BLOCK, imaginary)):
            high, low = split(value)
            factor_ref[section, top:bottom, first : first + BLOCK] = high
            factor_ref[section, top:bottom, 256 + first : 256 + first + BLOCK] = low
            factor_ref[section, top:bottom, 512 + first : 512 + first + BLOCK] = high

    for section in range(2):
        length = tile_of(length_ref[section])
        sigma = number * length * 0.25
        size = 0.0625 + sigma * sigma
        square = number * number / size
        z = (-0.0625 * square, -0.25 * sigma * square)
        sinh = c_sqrt(z)
        cosh = c_sqrt((1.0 + z[0], z[1]))
        root = (cosh[0] - sinh[0], cosh[1] - sinh[1])
        base = c_mul(root, root)
        gamma = c_mul((-2.0 * sigma * sigma / size, -0.5 * sigma / size), c_div(sinh, cosh))
        alpha = ((0.0625 - sigma * sigma) / size, 0.5 * sigma / size)
        turn = c_mul(alpha, alpha)
        hop = base
        for _ in range(7):
            hop = c_mul(hop, hop)
        whole = hop
        for _ in range(total.bit_length() - 8):
            whole = c_mul(whole, whole)
        close = c_div((jnp.ones_like(whole[0]), jnp.zeros_like(whole[0])), (1.0 - whole[0], -whole[1]))
        wide = spread_to(base, tall)
        gain = spread_to(gamma, tall)
        real, imaginary = c_mul(gain, grid_power(wide, jnp.abs(place - across), 7))
        real = real + jnp.where(place == across, 1.0, 0.0)
        keep(section, 0, 128, real, -imaginary)
        keep(section, 128, 256, imaginary, real)
        ahead = grid_power(base, lane, 7)
        behind = grid_power(base, 127 - lane, 7)
        left = c_mul(gamma, behind)
        right = c_mul(gamma, ahead)
        row = lax.broadcasted_iota(jnp.int32, (16, BLOCK), 0)

        def four(values):
            out = jnp.zeros((16, BLOCK), F32)
            for index, value in enumerate(values):
                out = jnp.where(row == index, jnp.broadcast_to(value[0:1], (16, BLOCK)), out)
            return out

        keep(section, 256, 272, four((left[0], left[1], right[0], right[1])), four((-left[1], left[0], -right[1], right[0])))
        factor_ref[section, 272:384, :] = jnp.zeros((112, 768), BF16)
        phase = number * length * jnp.broadcast_to(pad_ref[section : section + 1, :], (8, BLOCK))
        screen = c_mul(turn, (jnp.cos(phase), jnp.sin(phase)))
        reach_left = c_mul(base, ahead)
        reach_right = c_mul(base, behind)
        both = c_mul(gamma, hop)
        listed = [*screen, *lens, *reach_left, *reach_right, *hop, *close, *both]
        for index, value in enumerate(listed):
            row_ref[section, 8 * index : 8 * index + 8, :] = value
        down = grid_power(wide, place, 7)
        up = grid_power(wide, 127 - place, 7)
        high = c_mul(wide, down)
        low = c_mul(wide, up)
        from_left = c_mul(gain, up)
        from_right = c_mul(gain, down)
        tables = [high, low, from_left, from_right, c_mul(from_left, low), c_mul(from_right, high)]
        for index, table in enumerate(tables):
            weight_ref[section, 2 * index] = table[0]
            weight_ref[section, 2 * index + 1] = table[1]
    for copy in copies:
        copy.wait()


def split(value):
    high = value.astype(BF16)
    return high, (value - high.astype(F32)).astype(BF16)


def put_operand(operand_ref, top, real, imaginary):
    size = real.shape[0]
    high, low = split(real)
    operand_ref[top : top + size, 0:128] = high
    operand_ref[top : top + size, 256:384] = low
    high, low = split(imaginary)
    operand_ref[top : top + size, 128:256] = high
    operand_ref[top : top + size, 384:512] = low


def multiply(factor_ref, section, operand_ref, count=LHS_ROWS):
    high = operand_ref[:, 0:256]
    right = jnp.concatenate([high, high, operand_ref[:, 256:512]], axis=1)
    return lax.dot_general(factor_ref[section, 0:count, :], right, (((1,), (1,)), ((), ())), preferred_element_type=F32)


def reach_of(weight_ref, section, rows):
    return [weight_ref[section, index, rows, :] for index in range(4)]


def add_reach(table, value, line):
    high, low = table[0:2], table[2:4]
    return c_add(value, c_add(c_mul(high, (line[0], line[1])), c_mul(low, (line[2], line[3]))))


def line_of(carry_ref, block):
    return [carry_ref[block, part : part + 1, :] for part in range(4)]


def pick(table_ref, section, index, labels):
    table = jnp.broadcast_to(table_ref[section, 8 * index : 8 * index + 1, :], labels.shape)
    return jnp.take_along_axis(table, labels, axis=1, mode="promise_in_bounds")


def screen_at(row_ref, section, labels):
    return pick(row_ref, section, 0, labels), pick(row_ref, section, 1, labels)


def row_line(row_ref, section, index):
    return row_ref[section, 8 * index : 8 * index + 1, :]


def hop_of(row_ref, section):
    return (row_line(row_ref, section, 8), row_line(row_ref, section, 9)), (row_line(row_ref, section, 10), row_line(row_ref, section, 11))


def carries(get, put, count, hop, close):
    for reverse in (False, True):
        order = list(range(count))[:: -1 if reverse else 1]
        total = get(order[0], reverse)
        for index in order[1:]:
            total = c_add(c_mul(hop, total), get(index, reverse))
        carry = c_mul(close, total)
        for index in order:
            put(index, reverse, carry)
            carry = c_add(c_mul(hop, carry), get(index, reverse))


def scan_rows(edge_ref, carry_ref, row_ref, section, pairs):
    hop, close = hop_of(row_ref, section)

    def get(block, reverse):
        first = 2 if reverse else 0
        lanes = slice(128 * (block % 2), 128 * (block % 2) + 128)
        return tuple(edge_ref[block // 2, first + part : first + part + 1, lanes] for part in range(2))

    def put(block, reverse, value):
        for part in range(2):
            first = (2 if reverse else 0) + part
            carry_ref[block, first : first + 1, :] = value[part]

    carries(get, put, 2 * pairs, hop, close)


def row_finish(section, operand_ref, factor_ref, grid_ref, edge_ref, pair):
    out = multiply(factor_ref, section, operand_ref)
    grid_ref[pair] = out[0:256]
    edge_ref[pair] = out[256:264]


def column_stage(section, operand_ref, weight_ref, carry_ref, grid_ref, pair):
    lines = [line_of(carry_ref, 2 * pair + half) for half in range(2)]
    for top in range(0, BLOCK, CHUNK):
        rows = slice(top, top + CHUNK)
        table = reach_of(weight_ref, section, rows)
        for half in range(2):
            lanes = slice(128 * half, 128 * half + 128)
            value = (grid_ref[pair, rows, lanes], grid_ref[pair, top + BLOCK : top + BLOCK + CHUNK, lanes])
            put_operand(operand_ref, 128 * half + top, *add_reach(table, value, lines[half]))


def pack_edges(pair, ends, sums_ref):
    for half in range(2):
        sums_ref[2 * pair + half, 0:4, :] = ends[0:4, 128 * half : 128 * half + 128]


def pack_sums(section, out_ref, screen_ref, pair, row_ref, weight_ref, sums_ref):
    for half in range(2):
        block = 2 * pair + half
        lanes = lanes_of(pair, half)
        sums = [jnp.zeros((8, BLOCK), F32) for _ in range(10)]
        for top in range(0, BLOCK, 8):
            rows = slice(top, top + 8)
            screen = (screen_ref[0, rows, lanes], screen_ref[1, rows, lanes])
            value = c_mul(screen, (out_ref[0, rows, lanes], out_ref[1, rows, lanes]))
            weights = [(weight_ref[section, 2 * k, rows, :], weight_ref[section, 2 * k + 1, rows, :]) for k in range(2, 6)]
            terms = (c_mul(weights[0], value), c_mul(weights[1], value), screen, c_mul(weights[2], screen), c_mul(weights[3], screen))
            for k, term in enumerate(terms):
                sums[2 * k] = sums[2 * k] + term[0]
                sums[2 * k + 1] = sums[2 * k + 1] + term[1]
        lines = [jnp.sum(part, axis=0, keepdims=True) for part in sums]
        both = c_mul((row_line(row_ref, section, 12), row_line(row_ref, section, 13)), (lines[4], lines[5]))
        for k, line in enumerate(lines[0:4] + list(both) + lines[6:10]):
            sums_ref[block, 4 + k : 5 + k, :] = line
        sums_ref[block, 14:16, :] = jnp.zeros((2, BLOCK), F32)


def line_solve(section, back_ref, small_ref, line_ref, carry_ref, factor_ref, row_ref, blocks):
    small_ref[...] = jnp.zeros(small_ref.shape, F32)
    for block in range(blocks):
        for side in range(2):
            for part in range(2):
                row = 4 + 2 * side + part
                small_ref[8 * block + side : 8 * block + side + 1, 128 * part : 128 * part + 128] = back_ref[block, row : row + 1, :]
    high, low = split(small_ref[...])
    left = jnp.concatenate([high, high, low], axis=1)
    out = lax.dot_general(left, factor_ref[section], (((1,), (1,)), ((), ())), preferred_element_type=F32)
    line_ref[...] = out
    wide = (8, BLOCK)
    hop, close = (tuple(jnp.broadcast_to(part, wide) for part in pair) for pair in hop_of(row_ref, section))
    reach_left = tuple(row_ref[section, 8 * k : 8 * k + 8, :] for k in (4, 5))
    reach_right = tuple(row_ref[section, 8 * k : 8 * k + 8, :] for k in (6, 7))

    def get(block, reverse):
        first = 258 if reverse else 256
        rows = slice(8 * block, 8 * block + 8)
        return tuple(jnp.broadcast_to(line_ref[rows, first + part : first + part + 1], wide) for part in range(2))

    def put(block, reverse, value):
        rows = slice(8 * block, 8 * block + 8)
        add = c_mul(reach_right if reverse else reach_left, value)
        real = line_ref[rows, 0:128] + add[0]
        imaginary = line_ref[rows, 128:256] + add[1]
        if not reverse:
            line_ref[rows, 0:128] = real
            line_ref[rows, 128:256] = imaginary
        else:
            for side in range(2):
                carry_ref[block, 2 * side : 2 * side + 1, :] = real[side : side + 1]
                carry_ref[block, 2 * side + 1 : 2 * side + 2, :] = imaginary[side : side + 1]

    carries(get, put, blocks, hop, close)


def lanes_of(pair, half):
    return slice(256 * pair + 128 * half, 256 * pair + 128 * half + 128)


def wide_of(pair):
    return slice(256 * pair, 256 * pair + 256)


def steps(count, *bodies):
    for time in range(count + len(bodies) - 1):
        for depth, body in enumerate(bodies):
            if 0 <= time - depth < count:
                body(time - depth)


def first_kernel(pairs, field_ref, own_ref, other_ref, factor_ref, weight_ref, row_ref, out_ref, sums_ref, screen_ref,
                 operand_ref, grid_ref, edge_ref, carry_ref):
    labels = labels_of(0, own_ref, other_ref)

    def stage(pair):
        for half in range(2):
            lanes = lanes_of(pair, half)
            for top in range(0, BLOCK, CHUNK):
                rows = slice(top, top + CHUNK)
                screen = screen_at(row_ref, 0, labels(rows, lanes))
                screen_ref[0, rows, lanes] = screen[0]
                screen_ref[1, rows, lanes] = screen[1]
                value = c_mul(screen, (field_ref[0, rows, lanes], field_ref[1, rows, lanes]))
                put_operand(operand_ref.at[pair % SLOTS], 128 * half + top, *value)

    steps(pairs, stage, lambda pair: row_finish(0, operand_ref.at[pair % SLOTS], factor_ref, grid_ref, edge_ref, pair))
    scan_rows(edge_ref, carry_ref, row_ref, 0, pairs)

    def leave(pair):
        value = multiply(factor_ref, 0, operand_ref.at[pair % SLOTS])
        out_ref[0, :, wide_of(pair)] = value[0:128]
        out_ref[1, :, wide_of(pair)] = value[128:256]
        pack_edges(pair, value[256:264], sums_ref)

    steps(
        pairs,
        lambda pair: column_stage(0, operand_ref.at[pair % SLOTS], weight_ref, carry_ref, grid_ref, pair),
        leave,
        lambda pair: pack_sums(0, out_ref, screen_ref, pair, row_ref, weight_ref, sums_ref),
    )


def middle_kernel(peers, section, held_ref, row_ref, back_ref):
    hop, close = hop_of(row_ref, section)

    def line(peer, row):
        return held_ref[peer, row : row + 1, :], held_ref[peer, row + 1 : row + 2, :]

    def keep(first):
        def put(peer, reverse, value):
            row = first + (2 if reverse else 0)
            back_ref[peer, row : row + 1, :] = value[0]
            back_ref[peer, row + 1 : row + 2, :] = value[1]

        return put

    carries(lambda peer, reverse: line(peer, 2 if reverse else 0), keep(0), peers, hop, close)

    def later(peer, reverse):
        left = (back_ref[peer, 0:1, :], back_ref[peer, 1:2, :])
        right = (back_ref[peer, 2:3, :], back_ref[peer, 3:4, :])
        if reverse:
            return c_add(line(peer, 6), c_add(c_mul(line(peer, 12), left), c_mul(line(peer, 8), right)))
        return c_add(line(peer, 4), c_add(c_mul(line(peer, 8), left), c_mul(line(peer, 10), right)))

    carries(later, keep(4), peers, hop, close)


def labels_of(section, own_ref, other_ref):
    mine = lax.axis_index("sect")
    return lambda rows, lanes: jnp.where(mine == section, own_ref[0, rows, lanes], other_ref[0, rows, lanes])


def take_in(section, pair, value_in, screen_in, weight_ref, back_ref, operand_ref):
    lines = [line_of(back_ref, 2 * pair + half) for half in range(2)]
    for top in range(0, BLOCK, CHUNK):
        rows = slice(top, top + CHUNK)
        table = reach_of(weight_ref, section, rows)
        for half in range(2):
            lanes = lanes_of(pair, half)
            value = add_reach(table, (value_in[0, rows, lanes], value_in[1, rows, lanes]), lines[half])
            put_operand(operand_ref, 128 * half + top, *c_mul((screen_in[0, rows, lanes], screen_in[1, rows, lanes]), value))


def second_kernel(pairs, value_in, back_ref, screen_in, own_ref, other_ref, zone_ref, factor_ref, weight_ref, row_ref,
                  out_ref, sums_ref, screen_ref, operand_ref, grid_ref, edge_ref, carry_ref, late_ref, small_ref, line_ref, inner_ref):
    labels = labels_of(1, own_ref, other_ref)
    steps(
        pairs,
        lambda pair: take_in(0, pair, value_in, screen_in, weight_ref, back_ref, operand_ref.at[pair % SLOTS]),
        lambda pair: row_finish(0, operand_ref.at[pair % SLOTS], factor_ref, grid_ref, edge_ref, pair),
    )
    line_solve(0, back_ref, small_ref, line_ref, late_ref, factor_ref, row_ref, 2 * pairs)
    scan_rows(edge_ref, carry_ref, row_ref, 0, pairs)

    def turn(pair):
        out = multiply(factor_ref, 0, operand_ref.at[pair % SLOTS], 2 * BLOCK)
        lines = [line_of(late_ref, 2 * pair + half) for half in range(2)]
        for top in range(0, BLOCK, CHUNK):
            rows = slice(top, top + CHUNK)
            table = reach_of(weight_ref, 0, rows)
            for half in range(2):
                inner = slice(128 * half, 128 * half + 128)
                lanes = lanes_of(pair, half)
                value = (out[rows, inner], out[top + BLOCK : top + BLOCK + CHUNK, inner])
                value = add_reach(table, value, lines[half])
                screen = screen_at(row_ref, 1, labels(rows, lanes))
                screen_ref[0, rows, lanes] = screen[0]
                screen_ref[1, rows, lanes] = screen[1]
                zones = zone_ref[rows, lanes]
                value = c_mul((pick(row_ref, 1, 2, zones), pick(row_ref, 1, 3, zones)), c_mul(screen, value))
                put_operand(inner_ref.at[pair % SLOTS], 128 * half + top, *value)

    steps(
        pairs,
        lambda pair: column_stage(0, operand_ref.at[pair % SLOTS], weight_ref, carry_ref, grid_ref, pair),
        turn,
        lambda pair: row_finish(1, inner_ref.at[pair % SLOTS], factor_ref, grid_ref, edge_ref, pair),
    )
    scan_rows(edge_ref, carry_ref, row_ref, 1, pairs)

    def leave(pair):
        value = multiply(factor_ref, 1, operand_ref.at[pair % SLOTS])
        out_ref[0, :, wide_of(pair)] = value[0:128]
        out_ref[1, :, wide_of(pair)] = value[128:256]
        pack_edges(pair, value[256:264], sums_ref)

    steps(
        pairs,
        lambda pair: column_stage(1, operand_ref.at[pair % SLOTS], weight_ref, carry_ref, grid_ref, pair),
        leave,
        lambda pair: pack_sums(1, out_ref, screen_ref, pair, row_ref, weight_ref, sums_ref),
    )


def third_kernel(pairs, value_in, back_ref, screen_in, factor_ref, weight_ref, row_ref, out_any,
                 operand_ref, grid_ref, edge_ref, carry_ref, late_ref, small_ref, line_ref, out_ref, sems):
    def write(pair):
        wide = wide_of(pair)
        return pltpu.make_async_copy(out_ref.at[:, :, wide], out_any.at[0, :, :, wide], sems.at[pair])

    steps(
        pairs,
        lambda pair: take_in(1, pair, value_in, screen_in, weight_ref, back_ref, operand_ref.at[pair % SLOTS]),
        lambda pair: row_finish(1, operand_ref.at[pair % SLOTS], factor_ref, grid_ref, edge_ref, pair),
    )
    line_solve(1, back_ref, small_ref, line_ref, late_ref, factor_ref, row_ref, 2 * pairs)
    scan_rows(edge_ref, carry_ref, row_ref, 1, pairs)

    def leave(pair):
        out = multiply(factor_ref, 1, operand_ref.at[pair % SLOTS], 2 * BLOCK)
        lines = [line_of(late_ref, 2 * pair + half) for half in range(2)]
        for top in range(0, BLOCK, CHUNK):
            rows = slice(top, top + CHUNK)
            table = reach_of(weight_ref, 1, rows)
            for half in range(2):
                inner = slice(128 * half, 128 * half + 128)
                lanes = lanes_of(pair, half)
                value = (out[rows, inner], out[top + BLOCK : top + BLOCK + CHUNK, inner])
                value = add_reach(table, value, lines[half])
                out_ref[0, rows, lanes] = value[0]
                out_ref[1, rows, lanes] = value[1]
        write(pair).start()

    steps(pairs, lambda pair: column_stage(1, operand_ref.at[pair % SLOTS], weight_ref, carry_ref, grid_ref, pair), leave)
    for pair in range(pairs):
        write(pair).wait()


ANY = pl.BlockSpec(memory_space=pl.ANY)
VMEM = pl.BlockSpec(memory_space=pltpu.VMEM)
SMEM = pl.BlockSpec(memory_space=pltpu.SMEM)


def call(body, in_specs, out_shape, scratch=(), out_space=VMEM):
    out_specs = jax.tree.map(lambda _: out_space, out_shape)
    return pl.pallas_call(
        body,
        in_specs=in_specs,
        out_specs=out_specs,
        out_shape=out_shape,
        scratch_shapes=list(scratch),
        compiler_params=pltpu.CompilerParams(vmem_limit_bytes=VMEM_LIMIT),
        interpret=INTERPRET,
    )


def shape(*sizes, kind=F32):
    return jax.ShapeDtypeStruct(sizes, kind)


def kernels(peers, width):
    pairs = width // 256
    passing = [
        pltpu.VMEM((SLOTS, 256, 512), BF16),
        pltpu.VMEM((pairs, 256, 256), F32),
        pltpu.VMEM((pairs, 8, 256), F32),
        pltpu.VMEM((2 * pairs, 8, BLOCK), F32),
    ]
    small = [pltpu.VMEM((2 * pairs, 8, BLOCK), F32), pltpu.VMEM((16 * pairs, 256), F32), pltpu.VMEM((16 * pairs, 384), F32)]
    grid = shape(2, BLOCK, width)
    grids = (grid, shape(peers, 16, BLOCK), grid)
    prepare = call(
        partial(prepare_kernel, width),
        [SMEM, SMEM, VMEM, VMEM, ANY, ANY],
        (
            shape(2, 384, 768, kind=BF16), shape(2, 12, BLOCK, BLOCK), shape(2, 8 * 14, BLOCK),
            grid, shape(1, BLOCK, width, kind=jnp.int32),
        ),
        [pltpu.VMEM((8, BLOCK), F32), pltpu.SemaphoreType.DMA((2,))],
    )
    first = call(partial(first_kernel, pairs), [VMEM] * 6, grids, passing)
    middle = [call(partial(middle_kernel, peers, section), [VMEM, VMEM], shape(peers, 8, BLOCK)) for section in range(2)]
    second = call(partial(second_kernel, pairs), [VMEM] * 9, grids, passing + small + passing[:1])
    third = call(partial(third_kernel, pairs), [VMEM] * 6, shape(1, 2, BLOCK, width),
                 passing + small + [pltpu.VMEM((2, BLOCK, width), F32), pltpu.SemaphoreType.DMA((pairs,))], ANY)
    return prepare, first, middle, second, third


def stay(value):
    return value if INTERPRET else pltpu.with_memory_space_constraint(value, pltpu.HBM)


def fast_shards(fields, region_ids, index_offsets, step_lengths, wave_numbers, zone_ids, zone_phases):
    prepare, first, middle, second, third = kernels(lax.axis_size("slab"), fields.shape[-1])
    other = lax.ppermute(region_ids, "sect", [(0, 1), (1, 0)])
    small = [stay(table) for table in (wave_numbers, step_lengths, index_offsets, zone_phases)]
    factor, weights, row, field, own = prepare(*small, stay(fields), stay(region_ids))

    def exchange(sums, section):
        held = lax.all_to_all(sums, "slab", 0, 0, tiled=True)
        return lax.all_to_all(middle[section](held, row), "slab", 0, 0, tiled=True)

    value, sums, screen = first(field, own, other, factor, weights, row)
    back = exchange(sums, 0)
    value, sums, screen = second(value, back, screen, own, other, zone_ids, factor, weights, row)
    back = exchange(sums, 1)
    return third(value, back, screen, factor, weights, row)


def choose(fields, *others):
    rows, width = fields.shape[-2:]
    if rows == BLOCK and width == BLOCK * lax.axis_size("slab") and lax.axis_size("sect") == 2:
        return fast_shards(fields, *others)
    return shards(fields, *others)


def solution(mesh):
    return jax.shard_map(
        choose,
        mesh=mesh,
        in_specs=(
            P(None, None, "slab", None),
            P("sect", "slab", None),
            P(),
            P(),
            P(),
            P("slab", None),
            P(),
        ),
        out_specs=P("sect", None, "slab", None),
        check_vma=False,
    )
```
